128 devices in a mesh: row: 16 (over z, x), mp: 8 (over y, core).
Axes of the slice: x: 4, y: 4, z: 4, core: 2. Of those that a mesh axis runs over, the one named last changes fastest.
Arguments:
- token_ids: int32 [128, 128], P('row'), may hold values from 0 to 511
- set_lengths: int32 [128], P('row'), may hold values from 32 to 128
- live_counts: int32 [16], replicated, may hold values from 1 to 8, 64 in all
- embed_table: bfloat16 [512, 5120], replicated, may hold values from -3 to 3
- position_table: bfloat16 [128, 5120], replicated, may hold values from -3 to 3
- norm_gain: float32 [5120], replicated, may hold values from 0.1 to 1.9
- w_query: bfloat16 [5120, 5120], P('row', 'mp')
- w_key: bfloat16 [5120, 5120], P('row', 'mp')
- w_value: bfloat16 [5120, 5120], P('row', 'mp'), may hold values from -0.078125 to 0.078125
- w_out: bfloat16 [5120, 5120], P('mp', 'row'), may hold values from -0.078125 to 0.078125
Outputs:
- verified: bfloat16 [128, 128, 5120], P('row', None, 'mp')
The draws below stay inside these ranges and needn't reach their ends.
Inputs may be any that keep to these rules, and one draw needn't show every extreme that they name: Owner group g has live_counts[g] live sets, its first slots; the counts sum to 64 and one group holds 8. `set_lengths`: positions at or past a set's length are padding.
All inputs are finite; a program needn't handle non-finite values.
Results may differ from the reference program's by a relative error of at most 0.017.
Values may be sent and summed in bfloat16 or wider, within the bound.
No kernel may reach another device: no remote copies, remote signals or barrier semaphores. Data moves between devices by JAX's collectives and lax.ppermute only.
A program may use at most 128 MiB of HBM per device.

```python
import math
import jax
import jax.numpy as jnp
import numpy as np
from jax import lax

D = 5120
DH = 128
VOCAB = 512
SEQ = 128
SLOTS = 8
GROUPS = 16
SETS = 128
N_MP = 8


def shared_base(key):
    raw = jax.random.normal(jax.random.fold_in(key, 101), (D, D), jnp.float32)
    return jnp.clip(raw, -4.0, 4.0) * D ** (-0.5)


def draw_w_query(key, part):
    return shared_base(key).astype(jnp.bfloat16)


def draw_w_key(key, part):
    fresh = jnp.clip(jax.random.normal(jax.random.fold_in(key, 202), (D, D), jnp.float32), -4.0, 4.0) * D ** (-0.5)
    mixed_weight = fresh
    return mixed_weight.astype(jnp.bfloat16)


def place_ends(drawn, own_key, low, largest):
    shape = drawn.shape
    place = [jax.random.randint(jax.random.fold_in(own_key, axis), (), 0, shape[axis]) for axis in range(len(shape))]
    drawn = drawn.at[tuple(place)].set(low)
    longest = shape.index(max(shape))
    place[longest] = (place[longest] + 1) % shape[longest]
    return drawn.at[tuple(place)].set(largest)


def levels(key, shape, cuts, smallest, top_value):
    def one(position, shards_of):
        draws = jax.random.uniform(jax.random.fold_in(jax.random.fold_in(key, 6), position), (shards_of,), jnp.float32, smallest / len(cuts), top_value / len(cuts))
        return jnp.repeat(jnp.exp(draws), shape[position] // shards_of).reshape((-1,) + (1,) * (len(shape) - position - 1))

    gain = one(*cuts[0])
    for cut in cuts[1:]:
        gain = gain * one(*cut)
    return gain


def cumulative_ranks(amount, lean):
    loads = [(1 << 20) // math.isqrt(standing ** lean) + 1 for standing in range(1, amount + 1)]
    scale = 1 + sum(loads) // (1 << 30)
    return np.cumsum(np.array([max(1, weight // scale) for weight in loads]))


def skewed_ids(rng, dims, count, slope):
    grid = cumulative_ranks(count, slope)
    lot = jax.random.randint(jax.random.fold_in(rng, 1), dims, 0, int(grid[count - 1]))
    standing = jnp.searchsorted(jnp.asarray(grid, jnp.int32), lot, side="right")
    return jax.random.permutation(jax.random.fold_in(rng, 2), count)[standing].astype(jnp.int32)


def split_up(number_of, total, reach, skew):
    loads = [(1 << 20) // math.isqrt(grade ** skew) + 1 for grade in range(2, number_of + 1)]
    surplus, counts = total - reach - (number_of - 1), [1] * (number_of - 1)
    while surplus > 0:
        candidates = [i for i in range(number_of - 1) if counts[i] < reach]
        mass, budget = sum([loads[i] for i in candidates]), surplus
        for i in candidates:
            more = min(reach - counts[i], max(1, budget * loads[i] // mass), surplus)
            counts[i] = counts[i] + more
            surplus = surplus - more
    return np.array([reach] + counts)


def ragged_sizes(own_key, amount, total, bound, slope):
    if amount == 2:
        one = jax.random.randint(own_key, (), max(1, total - bound), min(bound, total - 1) + 1)
        return jnp.stack([one, total - one])
    sizes = jnp.asarray(split_up(amount, total, bound, slope), jnp.int32)
    twos = (amount - 1) // 2
    giver, sink = sizes[1:1 + 2 * twos:2], sizes[2:2 + 2 * twos:2]
    slack = jnp.minimum(giver - 1, bound - sink)
    passed = jax.random.randint(jax.random.fold_in(own_key, 1), (twos,), 0, 1 << 20) % (slack + 1)
    sizes = sizes.at[1:1 + 2 * twos:2].set(giver - passed).at[2:2 + 2 * twos:2].set(sink + passed)
    return sizes[jax.random.permutation(jax.random.fold_in(own_key, 2), amount)]


def noise(key, shape, spread, reach, cuts=(), held_as=jnp.bfloat16):
    result = jax.random.normal(key, shape, jnp.float32) * spread
    if len(cuts) > 0:
        result = levels(key, shape, cuts, -0.22, 0.18) * result
    return jnp.clip(result, min=-reach, max=reach).astype(held_as)


def setup_inputs(seed: int = 0) -> dict:
    arg_keys = jax.random.split(jax.random.key(seed), 11)
    return {
        "token_ids": place_ends(skewed_ids(arg_keys[0], (SETS, SEQ), VOCAB, 2), jax.random.fold_in(arg_keys[0], 3), 0, VOCAB - 1).astype(jnp.int32),
        "set_lengths": place_ends(jax.random.randint(arg_keys[1], (SETS,), SEQ // 4, SEQ + 1), jax.random.fold_in(arg_keys[1], 1), SEQ // 4, SEQ).astype(jnp.int32),
        "live_counts": ragged_sizes(arg_keys[2], GROUPS, GROUPS * SLOTS // 2, SLOTS, 2).astype(jnp.int32),
        "embed_table": noise(arg_keys[3], (VOCAB, D), 0.5, 3.0),
        "position_table": noise(arg_keys[4], (SEQ, D), 0.5, 3.0),
        "norm_gain": jnp.clip(1.0 + 0.18 * jax.random.normal(arg_keys[5], (D,), jnp.float32), 0.1, 1.9),
        "w_query": draw_w_query(jax.random.fold_in(arg_keys[10], 71), 0),
        "w_key": draw_w_key(jax.random.fold_in(arg_keys[10], 71), 0),
        "w_value": noise(arg_keys[8], (D, D), D ** -0.5, 0.078125, ((0, 16), (1, 8))),
        "w_out": noise(arg_keys[9], (D, D), D ** -0.5, 0.078125, ((0, 8), (1, 16))),
    }


def prepare(group_ids, embed_table, position_table, norm_gain):
    summed = jnp.take(embed_table, group_ids, axis=0).astype(jnp.float32) + position_table.astype(jnp.float32)[None]
    stored = lax.optimization_barrier(summed.astype(jnp.bfloat16))
    widened = stored.astype(jnp.float32)
    inverse = lax.rsqrt(lax.optimization_barrier(jnp.mean(widened * widened, axis=-1, keepdims=True)) + 1e-05)
    normed = (widened * inverse * norm_gain).astype(jnp.bfloat16)
    return (stored, normed)

def attend(query, keys, values, group_lengths, head_size):
    set_count = group_lengths.shape[0]
    seq_len = query.shape[0] // set_count
    q_four = query.astype(jnp.float32).reshape(set_count, seq_len, -1, head_size)
    k_four = keys.astype(jnp.float32).reshape(set_count, seq_len, -1, head_size)
    v_four = values.astype(jnp.float32).reshape(set_count, seq_len, -1, head_size)
    scores = jnp.einsum('sqhd,skhd->shqk', q_four, k_four) * head_size ** (-0.5)
    valid = jnp.arange(seq_len)[None, :] < group_lengths[:, None]
    scores = jnp.where(valid[:, None, None, :], scores, -1e+30)
    highest = lax.optimization_barrier(jnp.max(scores, axis=-1, keepdims=True))
    expo = jnp.exp(scores - highest)
    weights = (expo / lax.optimization_barrier(jnp.sum(expo, axis=-1, keepdims=True))).astype(jnp.bfloat16)
    mixed = jnp.einsum('shqk,skhd->sqhd', weights.astype(jnp.float32), v_four)
    return mixed.astype(jnp.bfloat16).reshape(set_count * seq_len, -1)

def reference(token_ids, set_lengths, live_counts, embed_table, position_table, norm_gain, w_query, w_key, w_value, w_out):

    def one_group(block):
        group_ids, group_lengths, group_count = block
        stored, normed = prepare(group_ids, embed_table, position_table, norm_gain)
        flat = normed.reshape(-1, D)
        query = jnp.dot(flat, w_query, preferred_element_type=jnp.float32).astype(jnp.bfloat16)
        keys = jnp.dot(flat, w_key, preferred_element_type=jnp.float32).astype(jnp.bfloat16)
        values = jnp.dot(flat, w_value, preferred_element_type=jnp.float32).astype(jnp.bfloat16)
        mixed = attend(query, keys, values, group_lengths, DH)
        split = mixed.astype(jnp.float32).reshape(-1, N_MP, D // N_MP)
        out_blocks = w_out.astype(jnp.float32).reshape(N_MP, D // N_MP, D)
        partial_value = jnp.einsum('tmk,mkd->tmd', split, out_blocks)
        rounded = lax.optimization_barrier(partial_value.astype(jnp.bfloat16)).astype(jnp.float32)
        total = lax.optimization_barrier(jnp.sum(rounded, axis=1))
        live = jnp.arange(SLOTS) < group_count
        valid = jnp.arange(SEQ)[None, :] < group_lengths[:, None]
        keep = (live[:, None] & valid).reshape(-1, 1).astype(jnp.float32)
        output = ((stored.reshape(-1, D).astype(jnp.float32) + total) * keep).astype(jnp.bfloat16)
        return output.reshape(SLOTS, SEQ, D)
    blocks = (token_ids.reshape(GROUPS, SLOTS, SEQ), set_lengths.reshape(GROUPS, SLOTS), live_counts)
    return lax.map(one_group, blocks).reshape(SETS, SEQ, D)
```

```python
import jax
import jax.numpy as jnp
from jax import lax
from jax.experimental import pallas as pl
from jax.experimental.pallas import tpu as pltpu
from jax.sharding import PartitionSpec as P

D = 5120
DH = 128
HEADS = 5
ROWS = 16
VOCAB = 512
SEQ = 128
SLOTS = 8
TABLE = VOCAB + SEQ
BLOCK = D // ROWS
FEATURES = 640
PART_A = 128
PART_B = BLOCK - PART_A
F32 = jnp.float32
BF16 = jnp.bfloat16
VMEM = 32 << 20


def mm(a, b, dims):
    return lax.dot_general(a, b, (dims, ((), ())), preferred_element_type=F32)


def table_kernel(e_ref, p_ref, w_ref, t_ref, r_ref, t_acc, g_acc, ee_acc, pp_acc):
    step = pl.program_id(0)

    @pl.when(step == 0)
    def _():
        t_acc[...] = jnp.zeros_like(t_acc)
        g_acc[...] = jnp.zeros_like(g_acc)
        ee_acc[...] = jnp.zeros_like(ee_acc)
        pp_acc[...] = jnp.zeros_like(pp_acc)

    e, p = e_ref[...], p_ref[...]
    w = w_ref[...].reshape(2 * BLOCK, DH)
    t_acc[:VOCAB] += mm(e, w, ((1,), (0,)))
    t_acc[VOCAB:] += mm(p, w, ((1,), (0,)))
    g_acc[...] += mm(e, p, ((1,), (1,)))
    pp_acc[...] += mm(p, p, ((1,), (1,)))
    wide = e.astype(F32)
    square = wide * wide
    folded = square[:, :128]
    for k in range(1, 2 * BLOCK // 128):
        folded += square[:, 128 * k : 128 * (k + 1)]
    ee_acc[...] += folded

    @pl.when(step == pl.num_programs(0) - 1)
    def _():
        t_ref[...] = t_acc[...].T.astype(BF16)
        ee = jnp.sum(ee_acc[...], axis=1, keepdims=True)
        diagonal = lax.broadcasted_iota(jnp.int32, (SEQ, SEQ), 0) == lax.broadcasted_iota(
            jnp.int32, (SEQ, SEQ), 1
        )
        pp = jnp.sum(jnp.where(diagonal, pp_acc[...], 0.0), axis=0, keepdims=True)
        total = jnp.maximum(ee + 2.0 * g_acc[...] + pp, 0.0)
        r_ref[...] = lax.rsqrt(total * (1.0 / D) + 1e-05)


def project_tables(embed_table, position_table, w_block):
    return pl.pallas_call(
        table_kernel,
        grid=(ROWS // 2,),
        in_specs=[
            pl.BlockSpec((VOCAB, 2 * BLOCK), lambda k: (0, k)),
            pl.BlockSpec((SEQ, 2 * BLOCK), lambda k: (0, k)),
            pl.BlockSpec((2, BLOCK, DH), lambda k: (k, 0, 0)),
        ],
        out_specs=[
            pl.BlockSpec((DH, TABLE), lambda k: (0, 0)),
            pl.BlockSpec((VOCAB, SEQ), lambda k: (0, 0)),
        ],
        out_shape=[
            jax.ShapeDtypeStruct((DH, TABLE), BF16),
            jax.ShapeDtypeStruct((VOCAB, SEQ), F32),
        ],
        scratch_shapes=[
            pltpu.VMEM((TABLE, DH), F32),
            pltpu.VMEM((VOCAB, SEQ), F32),
            pltpu.VMEM((VOCAB, 128), F32),
            pltpu.VMEM((SEQ, SEQ), F32),
        ],
        compiler_params=pltpu.CompilerParams(vmem_limit_bytes=VMEM),
        name="project_tables",
    )(embed_table, position_table, w_block)


def attend_kernel(lens_ref, live_ref, ids_ref, r_ref, t_ref, out_ref):
    step = pl.program_id(0)

    @pl.when(2 * step >= live_ref[0])
    def _():
        out_ref[...] = jnp.zeros_like(out_ref)

    @pl.when(2 * step < live_ref[0])
    def _():
        vocab = lax.broadcasted_iota(jnp.int32, (VOCAB, SEQ), 0)
        eye = lax.broadcasted_iota(jnp.int32, (SEQ, SEQ), 0) == lax.broadcasted_iota(
            jnp.int32, (SEQ, SEQ), 1
        )
        picks, scales = [], []
        for s in range(2):
            hit = vocab == ids_ref[pl.ds(2 * step + s, 1), :]
            scales.append(jnp.sum(jnp.where(hit, r_ref[...], 0.0), axis=0, keepdims=True))
            picks.append(
                jnp.concatenate(
                    [jnp.where(hit, 1.0, 0.0).astype(BF16), jnp.where(eye, 1.0, 0.0).astype(BF16)], 0
                )
            )
        pick = jnp.concatenate(picks, axis=1)
        scale = jnp.concatenate(scales, axis=1)
        table = t_ref[...].reshape(ROWS * DH, TABLE)
        rows = (mm(table[: 15 * DH], pick, ((1,), (0,))) * scale).astype(BF16)
        key_at = lax.broadcasted_iota(jnp.int32, (SEQ, SEQ), 0)
        for s in range(2):
            valid = key_at < lens_ref[2 * step + s]
            cols = slice(SEQ * s, SEQ * (s + 1))
            for h in range(HEADS):
                q = rows[DH * h : DH * (h + 1), cols]
                k = rows[DH * (HEADS + h) : DH * (HEADS + h + 1), cols]
                v = rows[DH * (2 * HEADS + h) : DH * (2 * HEADS + h + 1), cols]
                scores = mm(k, q, ((0,), (0,))) * DH ** (-0.5)
                scores = jnp.where(valid, scores, -1e30)
                expo = jnp.exp(scores - jnp.max(scores, axis=0, keepdims=True))
                weights = (expo / jnp.sum(expo, axis=0, keepdims=True)).astype(BF16)
                mixed = mm(v, weights, ((1,), (0,)))
                out_ref[cols, DH * h : DH * (h + 1)] = mixed.T.astype(BF16)


def attend(lengths, live, ids, r, tables):
    return pl.pallas_call(
        attend_kernel,
        grid_spec=pltpu.PrefetchScalarGridSpec(
            num_scalar_prefetch=2,
            grid=(SLOTS // 2,),
            in_specs=[
                pl.BlockSpec((SLOTS, SEQ), lambda i, *_: (0, 0)),
                pl.BlockSpec((VOCAB, SEQ), lambda i, *_: (0, 0)),
                pl.BlockSpec((ROWS, DH, TABLE), lambda i, *_: (0, 0, 0)),
            ],
            out_specs=pl.BlockSpec((2 * SEQ, FEATURES), lambda i, *_: (i, 0)),
        ),
        out_shape=jax.ShapeDtypeStruct((SLOTS * SEQ, FEATURES), BF16),
        compiler_params=pltpu.CompilerParams(vmem_limit_bytes=VMEM),
        name="attend",
    )(lengths, live, ids, r, tables)


def other_kernel(dest_ref, a_ref, w_ref, out_ref):
    w = w_ref[...].reshape(-1, FEATURES)
    out_ref[0] = mm(a_ref[...], w, ((1,), (1,))).astype(BF16)


def other_partials(dest, mixed, w):
    width = 2 * w.shape[1]
    tokens = mixed.shape[0]
    return pl.pallas_call(
        other_kernel,
        grid_spec=pltpu.PrefetchScalarGridSpec(
            num_scalar_prefetch=1,
            grid=(4,),
            in_specs=[
                pl.BlockSpec((tokens, FEATURES), lambda o, d: (0, 0)),
                pl.BlockSpec((2, width // 2, FEATURES), lambda o, d: (d[o], 0, 0)),
            ],
            out_specs=pl.BlockSpec((1, tokens, width), lambda o, d: (o, 0, 0)),
        ),
        out_shape=jax.ShapeDtypeStruct((4, tokens, width), BF16),
        compiler_params=pltpu.CompilerParams(vmem_limit_bytes=VMEM),
        name="other_partials",
    )(dest, mixed, w)


def own_kernel(dest_ref, a_ref, w0, w1, w2, w3, got_ref, *out_refs):
    for o, w_ref in enumerate((w0, w1, w2, w3)):
        w = w_ref[...].reshape(-1, FEATURES)
        part = mm(a_ref[...], w, ((1,), (1,))).astype(BF16).astype(F32)
        out_refs[o][...] = (part + got_ref[o].astype(F32)).astype(BF16)


def own_partials(dest, mixed, w, got):
    width = 2 * w.shape[1]
    tokens = mixed.shape[0]
    tile = 256

    def pick(o):
        return pl.BlockSpec((2, width // 2, FEATURES), lambda i, d: (d[o], 0, 0))

    return pl.pallas_call(
        own_kernel,
        grid_spec=pltpu.PrefetchScalarGridSpec(
            num_scalar_prefetch=1,
            grid=(tokens // tile,),
            in_specs=[
                pl.BlockSpec((tile, FEATURES), lambda i, d: (i, 0)),
                pick(0),
                pick(1),
                pick(2),
                pick(3),
                pl.BlockSpec((4, tile, width), lambda i, d: (0, i, 0)),
            ],
            out_specs=[pl.BlockSpec((tile, width), lambda i, d: (i, 0))] * 4,
        ),
        out_shape=[jax.ShapeDtypeStruct((tokens, width), BF16)] * 4,
        compiler_params=pltpu.CompilerParams(vmem_limit_bytes=VMEM),
        name="own_partials",
    )(dest, mixed, w, w, w, w, got)


def finish_kernel(lens_ref, live_ref, at_ref, ids_ref, e_ref, p_ref, *refs):
    a_refs, b_refs, out_ref = refs[:4], refs[4:8], refs[8]
    slot = pl.program_id(0)
    live = slot < live_ref[0]

    @pl.when(jnp.logical_not(live))
    def _():
        out_ref[...] = jnp.zeros_like(out_ref)

    @pl.when(live)
    def _():
        hit = lax.broadcasted_iota(jnp.int32, (VOCAB, SEQ), 0) == ids_ref[pl.ds(slot, 1), :]
        pick = jnp.where(hit, 1.0, 0.0).astype(BF16)
        stored = mm(pick, e_ref[...], ((0,), (0,))) + p_ref[...].astype(F32)
        stored = stored.astype(BF16).astype(F32)
        a = sum(ref[...].astype(F32) for ref in a_refs)
        b = sum(ref[...].astype(F32) for ref in b_refs)
        total = jnp.concatenate([a[:, :128], b[:, :256], a[:, 128:], b[:, 256:]], axis=1)
        valid = lax.broadcasted_iota(jnp.int32, (SEQ, FEATURES), 0) < lens_ref[slot]
        out_ref[0] = jnp.where(valid, stored + total, 0.0).astype(BF16)


def finish(lengths, live, at, ids, embed_table, position_table, a_parts, b_parts):
    part = [pl.BlockSpec((SEQ, x.shape[1]), lambda s, *_: (s, 0)) for x in (*a_parts, *b_parts)]
    return pl.pallas_call(
        finish_kernel,
        grid_spec=pltpu.PrefetchScalarGridSpec(
            num_scalar_prefetch=3,
            grid=(SLOTS,),
            in_specs=[
                pl.BlockSpec((SLOTS, SEQ), lambda s, *_: (0, 0)),
                pl.BlockSpec((VOCAB, FEATURES), lambda s, n, c, at: (0, at[0])),
                pl.BlockSpec((SEQ, FEATURES), lambda s, n, c, at: (0, at[0])),
                *part,
            ],
            out_specs=pl.BlockSpec((1, SEQ, FEATURES), lambda s, *_: (s, 0, 0)),
        ),
        out_shape=jax.ShapeDtypeStruct((SLOTS, SEQ, FEATURES), BF16),
        compiler_params=pltpu.CompilerParams(vmem_limit_bytes=VMEM),
        name="finish",
    )(lengths, live, at, ids, embed_table, position_table, *a_parts, *b_parts)


def on_device(
    token_ids,
    set_lengths,
    live_counts,
    embed_table,
    position_table,
    norm_gain,
    w_query,
    w_key,
    w_value,
    w_out,
):
    row = lax.axis_index("row")
    part = lax.axis_index("mp")
    y, core = part // 2, part % 2
    live = live_counts[row].reshape(1)

    turned = w_out.T
    odd = jnp.concatenate([turned[64:192], turned[:64], turned[192:]], axis=0)
    turned = jnp.where(row % 2 == 1, odd, turned)
    wa = lax.all_gather(turned[:PART_A], "row", axis=0)

    gain = lax.dynamic_slice_in_dim(norm_gain, row * BLOCK, BLOCK)[:, None]
    blocks = [
        (gain * w.astype(F32)).astype(BF16).reshape(BLOCK, HEADS, DH)
        for w in (w_query, w_key, w_value)
    ]
    packed = jnp.concatenate([*blocks, jnp.zeros((BLOCK, 1, DH), BF16)], axis=1)
    w_block = lax.all_to_all(packed.transpose(1, 0, 2), "row", 0, 0)

    mine, r = project_tables(embed_table, position_table, w_block)
    tables = lax.all_gather(mine, "row", axis=0)

    rest, tables = lax.optimization_barrier((turned[PART_A:], tables))
    wb = lax.all_gather(rest, "row", axis=0)

    mixed = attend(set_lengths, live, token_ids, r, tables)

    lines = (y + jnp.arange(4, dtype=jnp.int32)) % 4
    other = 2 * lines + 1 - core
    own = 2 * lines + core
    swap = [(2 * i + c, 2 * i + 1 - c) for i in range(4) for c in range(2)]

    def along(o):
        return [(2 * i + c, 2 * ((i + o) % 4) + c) for i in range(4) for c in range(2)]

    sums = []
    for w in (wa, wb):
        got = lax.ppermute(other_partials(other, mixed, w), "mp", swap)
        parts = own_partials(own, mixed, w, got)
        sums.append([parts[0]] + [lax.ppermute(parts[o], "mp", along(o)) for o in (1, 3, 2)])
    return finish(
        set_lengths,
        live,
        part.reshape(1),
        token_ids,
        embed_table,
        position_table,
        sums[0],
        sums[1],
    )


def solution(mesh):
    in_specs = (
        P("row", None),
        P("row"),
        P(),
        P(),
        P(),
        P(),
        P("row", "mp"),
        P("row", "mp"),
        P("row", "mp"),
        P("mp", "row"),
    )
    out_specs = P("row", None, "mp")
    return jax.shard_map(
        on_device, mesh=mesh, in_specs=in_specs, out_specs=out_specs, check_vma=False
    )
```

```python
import jax
import jax.numpy as jnp
from jax import lax
from jax.experimental import pallas as pl
from jax.experimental.pallas import tpu as pltpu
from jax.sharding import PartitionSpec as P

D = 5120
DH = 128
HEADS = 5
ROWS = 16
VOCAB = 512
SEQ = 128
SLOTS = 8
TABLE = VOCAB + SEQ
BLOCK = D // ROWS
FEATURES = 640
HALF = DH // 2
SIDE = 4
F32 = jnp.float32
BF16 = jnp.bfloat16
VMEM = 32 << 20


def mm(a, b, dims):
    return lax.dot_general(a, b, (dims, ((), ())), preferred_element_type=F32)


def table_kernel(e_ref, p_ref, w_ref, t_ref, r_ref, t_acc, g_acc, ee_acc, pp_acc):
    step = pl.program_id(0)

    @pl.when(step == 0)
    def _():
        t_acc[...] = jnp.zeros_like(t_acc)
        g_acc[...] = jnp.zeros_like(g_acc)
        ee_acc[...] = jnp.zeros_like(ee_acc)
        pp_acc[...] = jnp.zeros_like(pp_acc)

    e, p = e_ref[...], p_ref[...]
    w = w_ref[...].reshape(2 * BLOCK, DH)
    t_acc[:VOCAB] += mm(e, w, ((1,), (0,)))
    t_acc[VOCAB:] += mm(p, w, ((1,), (0,)))
    g_acc[...] += mm(e, p, ((1,), (1,)))
    pp_acc[...] += mm(p, p, ((1,), (1,)))
    wide = e.astype(F32)
    square = wide * wide
    folded = square[:, :128]
    for k in range(1, 2 * BLOCK // 128):
        folded += square[:, 128 * k : 128 * (k + 1)]
    ee_acc[...] += folded

    @pl.when(step == pl.num_programs(0) - 1)
    def _():
        t_ref[...] = t_acc[...].T.astype(BF16)
        ee = jnp.sum(ee_acc[...], axis=1, keepdims=True)
        diagonal = lax.broadcasted_iota(jnp.int32, (SEQ, SEQ), 0) == lax.broadcasted_iota(
            jnp.int32, (SEQ, SEQ), 1
        )
        pp = jnp.sum(jnp.where(diagonal, pp_acc[...], 0.0), axis=0, keepdims=True)
        total = jnp.maximum(ee + 2.0 * g_acc[...] + pp, 0.0)
        r_ref[...] = lax.rsqrt(total * (1.0 / D) + 1e-05)


def project_tables(embed_table, position_table, w_block):
    return pl.pallas_call(
        table_kernel,
        grid=(ROWS // 2,),
        in_specs=[
            pl.BlockSpec((VOCAB, 2 * BLOCK), lambda k: (0, k)),
            pl.BlockSpec((SEQ, 2 * BLOCK), lambda k: (0, k)),
            pl.BlockSpec((2, BLOCK, DH), lambda k: (k, 0, 0)),
        ],
        out_specs=[
            pl.BlockSpec((DH, TABLE), lambda k: (0, 0)),
            pl.BlockSpec((VOCAB, SEQ), lambda k: (0, 0)),
        ],
        out_shape=[
            jax.ShapeDtypeStruct((DH, TABLE), BF16),
            jax.ShapeDtypeStruct((VOCAB, SEQ), F32),
        ],
        scratch_shapes=[
            pltpu.VMEM((TABLE, DH), F32),
            pltpu.VMEM((VOCAB, SEQ), F32),
            pltpu.VMEM((VOCAB, 128), F32),
            pltpu.VMEM((SEQ, SEQ), F32),
        ],
        compiler_params=pltpu.CompilerParams(vmem_limit_bytes=VMEM),
        name="project_tables",
    )(embed_table, position_table, w_block)


def attend_kernel(lens_ref, live_ref, at_ref, ids_ref, r_ref, *refs):
    a_refs, b_refs, out_ref, table_ref = refs[:SIDE], refs[SIDE : 2 * SIDE], refs[-2], refs[-1]
    step = pl.program_id(0)
    z, x = at_ref[0] // SIDE, at_ref[0] % SIDE

    @pl.when(step == 0)
    def _():
        for dz in range(SIDE):
            for dx in range(SIDE):
                source = SIDE * ((z + SIDE - dz) % SIDE) + (x + SIDE - dx) % SIDE
                table_ref[pl.ds(source, 1), :HALF] = a_refs[dz][dx : dx + 1]
                table_ref[pl.ds(source, 1), HALF:] = b_refs[dx][dz : dz + 1]

    @pl.when(2 * step >= live_ref[0])
    def _():
        out_ref[...] = jnp.zeros_like(out_ref)

    @pl.when(2 * step < live_ref[0])
    def _():
        vocab = lax.broadcasted_iota(jnp.int32, (VOCAB, SEQ), 0)
        eye = lax.broadcasted_iota(jnp.int32, (SEQ, SEQ), 0) == lax.broadcasted_iota(
            jnp.int32, (SEQ, SEQ), 1
        )
        picks, scales = [], []
        for s in range(2):
            hit = vocab == ids_ref[pl.ds(2 * step + s, 1), :]
            scales.append(jnp.sum(jnp.where(hit, r_ref[...], 0.0), axis=0, keepdims=True))
            picks.append(
                jnp.concatenate(
                    [jnp.where(hit, 1.0, 0.0).astype(BF16), jnp.where(eye, 1.0, 0.0).astype(BF16)], 0
                )
            )
        pick = jnp.concatenate(picks, axis=1)
        scale = jnp.concatenate(scales, axis=1)
        table = table_ref[: 3 * HEADS].reshape(3 * HEADS * DH, TABLE)
        rows = (mm(table, pick, ((1,), (0,))) * scale).astype(BF16)
        key_at = lax.broadcasted_iota(jnp.int32, (SEQ, SEQ), 0)
        for s in range(2):
            valid = key_at < lens_ref[2 * step + s]
            cols = slice(SEQ * s, SEQ * (s + 1))
            for h in range(HEADS):
                q = rows[DH * h : DH * (h + 1), cols]
                k = rows[DH * (HEADS + h) : DH * (HEADS + h + 1), cols]
                v = rows[DH * (2 * HEADS + h) : DH * (2 * HEADS + h + 1), cols]
                scores = mm(k, q, ((0,), (0,))) * DH ** (-0.5)
                scores = jnp.where(valid, scores, -1e30)
                expo = jnp.exp(scores - jnp.max(scores, axis=0, keepdims=True))
                weights = (expo / jnp.sum(expo, axis=0, keepdims=True)).astype(BF16)
                mixed = mm(v, weights, ((1,), (0,)))
                out_ref[cols, DH * h : DH * (h + 1)] = mixed.T.astype(BF16)


def attend(lengths, live, at, ids, r, a_parts, b_parts):
    quarter = pl.BlockSpec((SIDE, HALF, TABLE), lambda i, *_: (0, 0, 0))
    return pl.pallas_call(
        attend_kernel,
        grid_spec=pltpu.PrefetchScalarGridSpec(
            num_scalar_prefetch=3,
            grid=(SLOTS // 2,),
            in_specs=[
                pl.BlockSpec((SLOTS, SEQ), lambda i, *_: (0, 0)),
                pl.BlockSpec((VOCAB, SEQ), lambda i, *_: (0, 0)),
                *[quarter] * (2 * SIDE),
            ],
            out_specs=pl.BlockSpec((2 * SEQ, FEATURES), lambda i, *_: (i, 0)),
            scratch_shapes=[pltpu.VMEM((ROWS, DH, TABLE), BF16)],
        ),
        out_shape=jax.ShapeDtypeStruct((SLOTS * SEQ, FEATURES), BF16),
        compiler_params=pltpu.CompilerParams(vmem_limit_bytes=VMEM),
        name="attend",
    )(lengths, live, at, ids, r, *a_parts, *b_parts)


def other_kernel(dest_ref, a_ref, w_ref, out_ref):
    w = w_ref[...].reshape(-1, FEATURES)
    out_ref[0] = mm(a_ref[...], w, ((1,), (1,))).astype(BF16)


def other_partials(dest, mixed, w):
    width = 2 * w.shape[1]
    tokens = mixed.shape[0]
    return pl.pallas_call(
        other_kernel,
        grid_spec=pltpu.PrefetchScalarGridSpec(
            num_scalar_prefetch=1,
            grid=(4,),
            in_specs=[
                pl.BlockSpec((tokens, FEATURES), lambda o, d: (0, 0)),
                pl.BlockSpec((2, width // 2, FEATURES), lambda o, d: (d[o], 0, 0)),
            ],
            out_specs=pl.BlockSpec((1, tokens, width), lambda o, d: (o, 0, 0)),
        ),
        out_shape=jax.ShapeDtypeStruct((4, tokens, width), BF16),
        compiler_params=pltpu.CompilerParams(vmem_limit_bytes=VMEM),
        name="other_partials",
    )(dest, mixed, w)


def far_kernel(dest_ref, a_ref, w_ref, got_ref, left_ref, right_ref):
    part = mm(a_ref[...], w_ref[...].reshape(-1, FEATURES), ((1,), (1,))).astype(BF16).astype(F32)
    total = (part + got_ref[0].astype(F32)).astype(BF16)
    left_ref[...] = total[:, : FEATURES // 2 + 64]
    right_ref[...] = total[:, FEATURES // 2 + 64 :]


def far_partials(dest, mixed, w, got):
    tokens, tile = mixed.shape[0], 256
    widths = (FEATURES // 2 + 64, FEATURES // 2 - 64)
    return pl.pallas_call(
        far_kernel,
        grid_spec=pltpu.PrefetchScalarGridSpec(
            num_scalar_prefetch=1,
            grid=(tokens // tile,),
            in_specs=[
                pl.BlockSpec((tile, FEATURES), lambda i, d: (i, 0)),
                pl.BlockSpec((2, BLOCK, FEATURES), lambda i, d: (d[2], 0, 0)),
                pl.BlockSpec((1, tile, FEATURES), lambda i, d: (2, i, 0)),
            ],
            out_specs=[pl.BlockSpec((tile, n), lambda i, d: (i, 0)) for n in widths],
        ),
        out_shape=[jax.ShapeDtypeStruct((tokens, n), BF16) for n in widths],
        compiler_params=pltpu.CompilerParams(vmem_limit_bytes=VMEM),
        name="far_partials",
    )(dest, mixed, w, got)


def near_kernel(dest_ref, a_ref, w_up, w_down, got_ref, got_down, from_below, from_above, up_ref, down_ref):
    cut = from_below.shape[1]
    up = mm(a_ref[...], w_up[...].reshape(-1, FEATURES), ((1,), (1,))).astype(BF16).astype(F32)
    up += got_ref[0].astype(F32)
    up_ref[:, :cut] = (up[:, :cut] + from_below[...].astype(F32)).astype(BF16)
    up_ref[:, cut:] = up[:, cut:].astype(BF16)
    down = mm(a_ref[...], w_down[...].reshape(-1, FEATURES), ((1,), (1,))).astype(BF16).astype(F32)
    down += got_down[0].astype(F32)
    down_ref[:, :cut] = down[:, :cut].astype(BF16)
    down_ref[:, cut:] = (down[:, cut:] + from_above[...].astype(F32)).astype(BF16)


def near_partials(dest, mixed, w, got, from_below, from_above):
    tokens, tile = mixed.shape[0], 256

    def pick(o):
        return pl.BlockSpec((2, BLOCK, FEATURES), lambda i, d: (d[o], 0, 0))

    def had(o):
        return pl.BlockSpec((1, tile, FEATURES), lambda i, d: (o, i, 0))

    def rows(n):
        return pl.BlockSpec((tile, n), lambda i, d: (i, 0))

    return pl.pallas_call(
        near_kernel,
        grid_spec=pltpu.PrefetchScalarGridSpec(
            num_scalar_prefetch=1,
            grid=(tokens // tile,),
            in_specs=[
                rows(FEATURES),
                pick(1),
                pick(3),
                had(1),
                had(3),
                rows(from_below.shape[1]),
                rows(from_above.shape[1]),
            ],
            out_specs=[rows(FEATURES)] * 2,
        ),
        out_shape=[jax.ShapeDtypeStruct((tokens, FEATURES), BF16)] * 2,
        compiler_params=pltpu.CompilerParams(vmem_limit_bytes=VMEM),
        name="near_partials",
    )(dest, mixed, w, w, got, got, from_below, from_above)


def finish_kernel(dest_ref, lens_ref, live_ref, at_ref, ids_ref, e_ref, p_ref, a_ref, w_ref, got_ref, below, above, out_ref):
    slot = pl.program_id(0)
    live = slot < live_ref[0]

    @pl.when(jnp.logical_not(live))
    def _():
        out_ref[...] = jnp.zeros_like(out_ref)

    @pl.when(live)
    def _():
        hit = lax.broadcasted_iota(jnp.int32, (VOCAB, SEQ), 0) == ids_ref[pl.ds(slot, 1), :]
        pick = jnp.where(hit, 1.0, 0.0).astype(BF16)
        stored = mm(pick, e_ref[...], ((0,), (0,))) + p_ref[...].astype(F32)
        stored = stored.astype(BF16).astype(F32)
        part = mm(a_ref[...], w_ref[...].reshape(-1, FEATURES), ((1,), (1,))).astype(BF16).astype(F32)
        total = part + got_ref[0].astype(F32) + below[...].astype(F32) + above[...].astype(F32)
        valid = lax.broadcasted_iota(jnp.int32, (SEQ, FEATURES), 0) < lens_ref[slot]
        out_ref[0] = jnp.where(valid, stored + total, 0.0).astype(BF16)


def finish(dest, lengths, live, at, ids, embed_table, position_table, mixed, w, got, below, above):
    rows = pl.BlockSpec((SEQ, FEATURES), lambda s, *_: (s, 0))
    return pl.pallas_call(
        finish_kernel,
        grid_spec=pltpu.PrefetchScalarGridSpec(
            num_scalar_prefetch=4,
            grid=(SLOTS,),
            in_specs=[
                pl.BlockSpec((SLOTS, SEQ), lambda s, *_: (0, 0)),
                pl.BlockSpec((VOCAB, FEATURES), lambda s, d, n, c, at: (0, at[0])),
                pl.BlockSpec((SEQ, FEATURES), lambda s, d, n, c, at: (0, at[0])),
                rows,
                pl.BlockSpec((2, BLOCK, FEATURES), lambda s, d, n, c, at: (d[0], 0, 0)),
                pl.BlockSpec((1, SEQ, FEATURES), lambda s, *_: (0, s, 0)),
                rows,
                rows,
            ],
            out_specs=pl.BlockSpec((1, SEQ, FEATURES), lambda s, *_: (s, 0, 0)),
        ),
        out_shape=jax.ShapeDtypeStruct((SLOTS, SEQ, FEATURES), BF16),
        compiler_params=pltpu.CompilerParams(vmem_limit_bytes=VMEM),
        name="finish",
    )(dest, lengths, live, at, ids, embed_table, position_table, mixed, w, got, below, above)


def on_device(
    token_ids,
    set_lengths,
    live_counts,
    embed_table,
    position_table,
    norm_gain,
    w_query,
    w_key,
    w_value,
    w_out,
):
    row = lax.axis_index("row")
    part = lax.axis_index("mp")
    y, core = part // 2, part % 2
    live = live_counts[row].reshape(1)

    w_all = lax.all_gather(w_out.T, "row", axis=0)

    gain = lax.dynamic_slice_in_dim(norm_gain, row * BLOCK, BLOCK)[:, None]
    blocks = [
        (gain * w.astype(F32)).astype(BF16).reshape(BLOCK, HEADS, DH)
        for w in (w_query, w_key, w_value)
    ]
    packed = jnp.concatenate([*blocks, jnp.zeros((BLOCK, 1, DH), BF16)], axis=1)
    w_block = lax.all_to_all(packed.transpose(1, 0, 2), "row", 0, 0)

    mine, r = project_tables(embed_table, position_table, w_block)

    def shifted(o, along_x):
        pairs = []
        for z in range(SIDE):
            for x in range(SIDE):
                to = SIDE * z + (x + o) % SIDE if along_x else SIDE * ((z + o) % SIDE) + x
                pairs.append((SIDE * z + x, to))
        return pairs

    def spread(value, along_x):
        near = {o: lax.ppermute(value, "row", shifted(o, along_x)) for o in (1, 3, 2)}
        return [value, near[1], near[2], near[3]]

    a_line = jnp.stack(spread(mine[:HALF], True))
    b_line = jnp.stack(spread(mine[HALF:], False))
    a_parts, b_parts = spread(a_line, False), spread(b_line, True)

    mixed = attend(set_lengths, live, row.reshape(1), token_ids, r, a_parts, b_parts)

    lines = (y + jnp.arange(SIDE, dtype=jnp.int32)) % SIDE
    other = 2 * lines + 1 - core
    own = 2 * lines + core
    swap = [(2 * i + c, 2 * i + 1 - c) for i in range(SIDE) for c in range(2)]

    def along(o):
        return [(2 * i + c, 2 * ((i + o) % SIDE) + c) for i in range(SIDE) for c in range(2)]

    got = lax.ppermute(other_partials(other, mixed, w_all), "mp", swap)
    left, right = far_partials(own, mixed, w_all, got)
    from_below = lax.ppermute(left, "mp", along(1))
    from_above = lax.ppermute(right, "mp", along(3))
    up, down = near_partials(own, mixed, w_all, got, from_below, from_above)
    below = lax.ppermute(up, "mp", along(1))
    above = lax.ppermute(down, "mp", along(3))
    return finish(
        own,
        set_lengths,
        live,
        part.reshape(1),
        token_ids,
        embed_table,
        position_table,
        mixed,
        w_all,
        got,
        below,
        above,
    )


def solution(mesh):
    in_specs = (
        P("row", None),
        P("row"),
        P(),
        P(),
        P(),
        P(),
        P("row", "mp"),
        P("row", "mp"),
        P("row", "mp"),
        P("mp", "row"),
    )
    out_specs = P("row", None, "mp")
    return jax.shard_map(
        on_device, mesh=mesh, in_specs=in_specs, out_specs=out_specs, check_vma=False
    )
```

```python
import jax
import jax.numpy as jnp
from jax import lax
from jax.experimental import pallas as pl
from jax.experimental.pallas import tpu as pltpu
from jax.sharding import PartitionSpec as P

D = 5120
DH = 128
HEADS = 5
ROWS = 16
VOCAB = 512
SEQ = 128
SLOTS = 8
TABLE = VOCAB + SEQ
BLOCK = D // ROWS
FEATURES = 640
HALF = DH // 2
SIDE = 4
F32 = jnp.float32
BF16 = jnp.bfloat16
VMEM = 16 << 20
NOTE = 16
GROUP = 16
CAPACITIES = (640, 704, 768, 832, 896, SLOTS * SEQ)


def mm(a, b, dims):
    return lax.dot_general(a, b, (dims, ((), ())), preferred_element_type=F32)


def pack_kernel(count_ref, gain_ref, q_ref, k_ref, v_ref, out_ref):
    gain = gain_ref[...]
    for j, ref in enumerate((q_ref, k_ref, v_ref)):
        for h in range(HEADS):
            block = gain * ref[:, DH * h : DH * (h + 1)].astype(F32)
            out_ref[HEADS * j + h, :BLOCK] = block.astype(BF16)
    out_ref[ROWS - 1, :BLOCK] = jnp.zeros((BLOCK, DH), BF16)
    count = jnp.full((NOTE, DH), count_ref[0], jnp.int32).astype(F32).astype(BF16)
    for i in range(ROWS):
        out_ref[i, BLOCK:] = count


def pack(count, gain, w_query, w_key, w_value):
    tile = pl.BlockSpec((BLOCK, FEATURES), lambda i, *_: (0, 0))
    return pl.pallas_call(
        pack_kernel,
        grid_spec=pltpu.PrefetchScalarGridSpec(
            num_scalar_prefetch=1,
            grid=(1,),
            in_specs=[pl.BlockSpec((BLOCK, 1), lambda i, *_: (0, 0)), tile, tile, tile],
            out_specs=pl.BlockSpec((ROWS, BLOCK + NOTE, DH), lambda i, *_: (0, 0, 0)),
        ),
        out_shape=jax.ShapeDtypeStruct((ROWS, BLOCK + NOTE, DH), BF16),
        compiler_params=pltpu.CompilerParams(vmem_limit_bytes=VMEM),
        name="pack",
    )(count, gain, w_query, w_key, w_value)


def table_kernel(e_ref, p_ref, w_ref, t_ref, t_acc):
    step = pl.program_id(0)

    @pl.when(step == 0)
    def _():
        t_acc[...] = jnp.zeros_like(t_acc)

    w = w_ref[:, :BLOCK].reshape(2 * BLOCK, DH)
    t_acc[:, :VOCAB] += mm(w, e_ref[...], ((0,), (1,)))
    t_acc[:, VOCAB:] += mm(w, p_ref[...], ((0,), (1,)))

    @pl.when(step == pl.num_programs(0) - 1)
    def _():
        t_ref[...] = t_acc[...].astype(BF16)


def project_tables(embed_table, position_table, w_block):
    return pl.pallas_call(
        table_kernel,
        grid=(ROWS // 2,),
        in_specs=[
            pl.BlockSpec((VOCAB, 2 * BLOCK), lambda k: (0, k)),
            pl.BlockSpec((SEQ, 2 * BLOCK), lambda k: (0, k)),
            pl.BlockSpec((2, BLOCK + NOTE, DH), lambda k: (k, 0, 0)),
        ],
        out_specs=pl.BlockSpec((DH, TABLE), lambda k: (0, 0)),
        out_shape=jax.ShapeDtypeStruct((DH, TABLE), BF16),
        scratch_shapes=[pltpu.VMEM((DH, TABLE), F32)],
        compiler_params=pltpu.CompilerParams(vmem_limit_bytes=VMEM),
        name="project_tables",
    )(embed_table, position_table, w_block)


def scale_kernel(e_ref, p_ref, r_ref, g_acc, ee_acc, pp_acc):
    step = pl.program_id(0)

    @pl.when(step == 0)
    def _():
        g_acc[...] = jnp.zeros_like(g_acc)
        ee_acc[...] = jnp.zeros_like(ee_acc)
        pp_acc[...] = jnp.zeros_like(pp_acc)

    e, p = e_ref[...], p_ref[...]
    g_acc[...] += mm(e, p, ((1,), (1,)))
    pp_acc[...] += mm(p, p, ((1,), (1,)))
    wide = e.astype(F32)
    square = wide * wide
    folded = square[:, :128]
    for k in range(1, 2 * BLOCK // 128):
        folded += square[:, 128 * k : 128 * (k + 1)]
    ee_acc[...] += folded

    @pl.when(step == pl.num_programs(0) - 1)
    def _():
        ee = jnp.sum(ee_acc[...], axis=1, keepdims=True)
        diagonal = lax.broadcasted_iota(jnp.int32, (SEQ, SEQ), 0) == lax.broadcasted_iota(
            jnp.int32, (SEQ, SEQ), 1
        )
        pp = jnp.sum(jnp.where(diagonal, pp_acc[...], 0.0), axis=0, keepdims=True)
        total = jnp.maximum(ee + 2.0 * g_acc[...] + pp, 0.0)
        r_ref[...] = lax.rsqrt(total * (1.0 / D) + 1e-05)


def norm_scales(embed_table, position_table):
    return pl.pallas_call(
        scale_kernel,
        grid=(ROWS // 2,),
        in_specs=[
            pl.BlockSpec((VOCAB, 2 * BLOCK), lambda k: (0, k)),
            pl.BlockSpec((SEQ, 2 * BLOCK), lambda k: (0, k)),
        ],
        out_specs=pl.BlockSpec((VOCAB, SEQ), lambda k: (0, 0)),
        out_shape=jax.ShapeDtypeStruct((VOCAB, SEQ), F32),
        scratch_shapes=[
            pltpu.VMEM((VOCAB, SEQ), F32),
            pltpu.VMEM((VOCAB, 128), F32),
            pltpu.VMEM((SEQ, SEQ), F32),
        ],
        compiler_params=pltpu.CompilerParams(vmem_limit_bytes=VMEM),
        name="norm_scales",
    )(embed_table, position_table)


def residual_kernel(live_ref, at_ref, ids_ref, e_ref, p_ref, out_ref):
    slot = pl.program_id(0)

    @pl.when(slot < live_ref[0])
    def _():
        hit = lax.broadcasted_iota(jnp.int32, (VOCAB, SEQ), 0) == ids_ref[pl.ds(slot, 1), :]
        pick = jnp.where(hit, 1.0, 0.0).astype(BF16)
        stored = mm(pick, e_ref[...], ((0,), (0,))) + p_ref[...].astype(F32)
        out_ref[0] = stored.astype(BF16)

    @pl.when(slot >= live_ref[0])
    def _():
        out_ref[...] = jnp.zeros_like(out_ref)


def residual(live, at, ids, embed_table, position_table):
    return pl.pallas_call(
        residual_kernel,
        grid_spec=pltpu.PrefetchScalarGridSpec(
            num_scalar_prefetch=2,
            grid=(SLOTS,),
            in_specs=[
                pl.BlockSpec((SLOTS, SEQ), lambda s, *_: (0, 0)),
                pl.BlockSpec((VOCAB, FEATURES), lambda s, c, at: (0, at[0])),
                pl.BlockSpec((SEQ, FEATURES), lambda s, c, at: (0, at[0])),
            ],
            out_specs=pl.BlockSpec((1, SEQ, FEATURES), lambda s, *_: (s, 0, 0)),
        ),
        out_shape=jax.ShapeDtypeStruct((SLOTS, SEQ, FEATURES), BF16),
        compiler_params=pltpu.CompilerParams(vmem_limit_bytes=VMEM),
        name="residual",
    )(live, at, ids, embed_table, position_table)


def attend_kernel(lens_ref, live_ref, at_ref, off_ref, ids_ref, r_ref, *refs):
    a_refs, b_refs = refs[:SIDE], refs[SIDE : 2 * SIDE]
    out_ref, table_ref, set_ref = refs[2 * SIDE :]
    step = pl.program_id(0)
    z, x = at_ref[0] // SIDE, at_ref[0] % SIDE

    @pl.when(step == 0)
    def _():
        for dz in range(SIDE):
            for dx in range(SIDE):
                source = SIDE * ((z + SIDE - dz) % SIDE) + (x + SIDE - dx) % SIDE
                table_ref[pl.ds(source, 1), :HALF] = a_refs[dz][dx : dx + 1]
                table_ref[pl.ds(source, 1), HALF:] = b_refs[dx][dz : dz + 1]
        out_ref[...] = jnp.zeros_like(out_ref)

    @pl.when(2 * step < live_ref[0])
    def _():
        vocab = lax.broadcasted_iota(jnp.int32, (VOCAB, SEQ), 0)
        eye = lax.broadcasted_iota(jnp.int32, (SEQ, SEQ), 0) == lax.broadcasted_iota(
            jnp.int32, (SEQ, SEQ), 1
        )
        picks, scales = [], []
        for s in range(2):
            hit = vocab == ids_ref[pl.ds(2 * step + s, 1), :]
            scales.append(jnp.sum(jnp.where(hit, r_ref[...], 0.0), axis=0, keepdims=True))
            picks.append(
                jnp.concatenate(
                    [jnp.where(hit, 1.0, 0.0).astype(BF16), jnp.where(eye, 1.0, 0.0).astype(BF16)], 0
                )
            )
        pick = jnp.concatenate(picks, axis=1)
        scale = jnp.concatenate(scales, axis=1)
        table = table_ref[: 3 * HEADS].reshape(3 * HEADS * DH, TABLE)
        rows = (mm(table, pick, ((1,), (0,))) * scale).astype(BF16)
        key_at = lax.broadcasted_iota(jnp.int32, (SEQ, SEQ), 0)
        for s in range(2):
            valid = key_at < lens_ref[2 * step + s]
            cols = slice(SEQ * s, SEQ * (s + 1))
            for h in range(HEADS):
                q = rows[DH * h : DH * (h + 1), cols]
                k = rows[DH * (HEADS + h) : DH * (HEADS + h + 1), cols]
                v = rows[DH * (2 * HEADS + h) : DH * (2 * HEADS + h + 1), cols]
                scores = mm(k, q, ((0,), (0,))) * DH ** (-0.5)
                scores = jnp.where(valid, scores, -1e30)
                expo = jnp.exp(scores - jnp.max(scores, axis=0, keepdims=True))
                weights = (expo / jnp.sum(expo, axis=0, keepdims=True)).astype(BF16)
                mixed = mm(v, weights, ((1,), (0,)))
                set_ref[s, :, DH * h : DH * (h + 1)] = mixed.T.astype(BF16)
        for s in range(2):
            for i in range(SEQ // GROUP):

                @pl.when((2 * step + s < live_ref[0]) & (GROUP * i < lens_ref[2 * step + s]))
                def _(s=s, i=i):
                    at = pl.multiple_of(off_ref[2 * step + s] + GROUP * i, GROUP)
                    out_ref[pl.ds(at, GROUP), :] = set_ref[s, GROUP * i : GROUP * (i + 1), :]


def attend(capacity, lengths, live, at, offsets, ids, r, a_parts, b_parts):
    quarter = pl.BlockSpec((SIDE, HALF, TABLE), lambda i, *_: (0, 0, 0))
    return pl.pallas_call(
        attend_kernel,
        grid_spec=pltpu.PrefetchScalarGridSpec(
            num_scalar_prefetch=4,
            grid=(SLOTS // 2,),
            in_specs=[
                pl.BlockSpec((SLOTS, SEQ), lambda i, *_: (0, 0)),
                pl.BlockSpec((VOCAB, SEQ), lambda i, *_: (0, 0)),
                *[quarter] * (2 * SIDE),
            ],
            out_specs=pl.BlockSpec((capacity, FEATURES), lambda i, *_: (0, 0)),
            scratch_shapes=[
                pltpu.VMEM((ROWS, DH, TABLE), BF16),
                pltpu.VMEM((2, SEQ, FEATURES), BF16),
            ],
        ),
        out_shape=jax.ShapeDtypeStruct((capacity, FEATURES), BF16),
        compiler_params=pltpu.CompilerParams(vmem_limit_bytes=24 << 20),
        name="attend",
    )(lengths, live, at, offsets, ids, r, *a_parts, *b_parts)


def partial_kernel(dest_ref, a_ref, w_ref, out_ref):
    out_ref[0] = mm(a_ref[...], w_ref[...].reshape(-1, FEATURES), ((1,), (1,))).astype(BF16)


def partials(dest, mixed, w):
    tokens, count = mixed.shape[0], dest.shape[0]
    return pl.pallas_call(
        partial_kernel,
        grid_spec=pltpu.PrefetchScalarGridSpec(
            num_scalar_prefetch=1,
            grid=(count,),
            in_specs=[
                pl.BlockSpec((tokens, FEATURES), lambda o, d: (0, 0)),
                pl.BlockSpec((2, BLOCK, FEATURES), lambda o, d: (d[o], 0, 0)),
            ],
            out_specs=pl.BlockSpec((1, tokens, FEATURES), lambda o, d: (o, 0, 0)),
        ),
        out_shape=jax.ShapeDtypeStruct((count, tokens, FEATURES), BF16),
        compiler_params=pltpu.CompilerParams(vmem_limit_bytes=VMEM),
        name="partials",
    )(dest, mixed, w)


def rounded_part(a_ref, w_ref):
    return mm(a_ref[...], w_ref[...].reshape(-1, FEATURES), ((1,), (1,))).astype(BF16).astype(F32)


def far_kernel(dest_ref, a_ref, w_ref, got_ref, top_ref, bottom_ref):
    half = pl.program_id(0)
    total = (rounded_part(a_ref, w_ref) + got_ref[0].astype(F32)).astype(BF16)

    @pl.when(half == 0)
    def _():
        top_ref[...] = total

    @pl.when(half == 1)
    def _():
        bottom_ref[...] = total


def far_partials(dest, mixed, w, got):
    tile = mixed.shape[0] // 2
    rows = pl.BlockSpec((tile, FEATURES), lambda i, d: (i, 0))
    whole = pl.BlockSpec((tile, FEATURES), lambda i, d: (0, 0))
    return pl.pallas_call(
        far_kernel,
        grid_spec=pltpu.PrefetchScalarGridSpec(
            num_scalar_prefetch=1,
            grid=(2,),
            in_specs=[
                rows,
                pl.BlockSpec((2, BLOCK, FEATURES), lambda i, d: (d[0], 0, 0)),
                pl.BlockSpec((1, tile, FEATURES), lambda i, d: (0, i, 0)),
            ],
            out_specs=[whole, whole],
        ),
        out_shape=[jax.ShapeDtypeStruct((tile, FEATURES), BF16)] * 2,
        compiler_params=pltpu.CompilerParams(vmem_limit_bytes=VMEM),
        name="far_partials",
    )(dest, mixed, w, got)


def near_kernel(dest_ref, a_ref, w_up, w_down, got_up, got_down, from_below, from_above, up_ref, down_ref):
    half = pl.program_id(0)
    up = rounded_part(a_ref, w_up) + got_up[0].astype(F32)
    down = rounded_part(a_ref, w_down) + got_down[0].astype(F32)

    @pl.when(half == 0)
    def _():
        up_ref[...] = (up + from_below[...].astype(F32)).astype(BF16)
        down_ref[...] = down.astype(BF16)

    @pl.when(half == 1)
    def _():
        up_ref[...] = up.astype(BF16)
        down_ref[...] = (down + from_above[...].astype(F32)).astype(BF16)


def near_partials(dest, mixed, w, got, from_below, from_above):
    tokens = mixed.shape[0]
    tile = tokens // 2
    rows = pl.BlockSpec((tile, FEATURES), lambda i, d: (i, 0))
    whole = pl.BlockSpec((tile, FEATURES), lambda i, d: (0, 0))

    def pick(o):
        return pl.BlockSpec((2, BLOCK, FEATURES), lambda i, d: (d[o], 0, 0))

    def had(o):
        return pl.BlockSpec((1, tile, FEATURES), lambda i, d: (o, i, 0))

    return pl.pallas_call(
        near_kernel,
        grid_spec=pltpu.PrefetchScalarGridSpec(
            num_scalar_prefetch=1,
            grid=(2,),
            in_specs=[rows, pick(0), pick(1), had(0), had(1), whole, whole],
            out_specs=[rows, rows],
        ),
        out_shape=[jax.ShapeDtypeStruct((tokens, FEATURES), BF16)] * 2,
        compiler_params=pltpu.CompilerParams(vmem_limit_bytes=VMEM),
        name="near_partials",
    )(dest, mixed, w, w, got, got, from_below, from_above)


def base_kernel(dest_ref, a_ref, w_ref, got_ref, out_ref):
    out_ref[...] = rounded_part(a_ref, w_ref) + got_ref[0].astype(F32)


def base_partial(dest, mixed, w, got):
    tokens = mixed.shape[0]
    tile = tokens // 2
    rows = pl.BlockSpec((tile, FEATURES), lambda i, d: (i, 0))
    return pl.pallas_call(
        base_kernel,
        grid_spec=pltpu.PrefetchScalarGridSpec(
            num_scalar_prefetch=1,
            grid=(2,),
            in_specs=[
                rows,
                pl.BlockSpec((2, BLOCK, FEATURES), lambda i, d: (d[2], 0, 0)),
                pl.BlockSpec((1, tile, FEATURES), lambda i, d: (2, i, 0)),
            ],
            out_specs=rows,
        ),
        out_shape=jax.ShapeDtypeStruct((tokens, FEATURES), F32),
        compiler_params=pltpu.CompilerParams(vmem_limit_bytes=VMEM),
        name="base_partial",
    )(dest, mixed, w, got)


def finish_kernel(lens_ref, live_ref, off_ref, stored_ref, base_ref, below_ref, above_ref, out_ref):
    slot = pl.program_id(0)
    for i in range(SEQ // GROUP):
        here = slice(GROUP * i, GROUP * (i + 1))
        live = (slot < live_ref[0]) & (GROUP * i < lens_ref[slot])

        @pl.when(live)
        def _(i=i, here=here):
            at = pl.ds(pl.multiple_of(off_ref[slot] + GROUP * i, GROUP), GROUP)
            total = base_ref[at, :] + below_ref[at, :].astype(F32) + above_ref[at, :].astype(F32)
            place = GROUP * i + lax.broadcasted_iota(jnp.int32, (GROUP, FEATURES), 0)
            result = stored_ref[0, here].astype(F32) + total
            out_ref[0, here] = jnp.where(place < lens_ref[slot], result, 0.0).astype(BF16)

        @pl.when(jnp.logical_not(live))
        def _(here=here):
            out_ref[0, here] = jnp.zeros((GROUP, FEATURES), BF16)


def finish(lengths, live, offsets, stored, base, below, above):
    whole = pl.BlockSpec(base.shape, lambda s, *_: (0, 0))
    one = pl.BlockSpec((1, SEQ, FEATURES), lambda s, *_: (s, 0, 0))
    return pl.pallas_call(
        finish_kernel,
        grid_spec=pltpu.PrefetchScalarGridSpec(
            num_scalar_prefetch=3,
            grid=(SLOTS,),
            in_specs=[one, whole, whole, whole],
            out_specs=one,
        ),
        out_shape=jax.ShapeDtypeStruct((SLOTS, SEQ, FEATURES), BF16),
        compiler_params=pltpu.CompilerParams(vmem_limit_bytes=VMEM),
        name="finish",
    )(lengths, live, offsets, stored, base, below, above)


def on_device(
    token_ids,
    set_lengths,
    live_counts,
    embed_table,
    position_table,
    norm_gain,
    w_query,
    w_key,
    w_value,
    w_out,
):
    row = lax.axis_index("row")
    part = lax.axis_index("mp")
    y, core = part // 2, part % 2
    live = live_counts[row].reshape(1)

    w_all = lax.all_gather(w_out.T, "row", axis=0)

    held = jnp.arange(SLOTS) < live[0]
    rows = jnp.where(held, (set_lengths + GROUP - 1) // GROUP, 0)
    before = jnp.arange(SLOTS)[:, None] > jnp.arange(SLOTS)[None]
    offsets = GROUP * jnp.sum(jnp.where(before, rows[None], 0), axis=1)

    gain = lax.dynamic_slice_in_dim(norm_gain, row * BLOCK, BLOCK)[:, None]
    packed = pack(jnp.sum(rows).reshape(1), gain, w_query, w_key, w_value)
    w_block = lax.all_to_all(packed, "row", 0, 0)
    most = GROUP * jnp.max(w_block[:, BLOCK, 0].astype(F32)).astype(jnp.int32)
    mine = project_tables(embed_table, position_table, w_block)
    r = norm_scales(embed_table, position_table)
    stored = residual(live, part.reshape(1), token_ids, embed_table, position_table)

    def shifted(o, along_x):
        pairs = []
        for z in range(SIDE):
            for x in range(SIDE):
                to = SIDE * z + (x + o) % SIDE if along_x else SIDE * ((z + o) % SIDE) + x
                pairs.append((SIDE * z + x, to))
        return pairs

    def spread(value, along_x):
        near = {o: lax.ppermute(value, "row", shifted(o, along_x)) for o in (1, 3, 2)}
        return [value, near[1], near[2], near[3]]

    a_line = jnp.stack(spread(mine[:HALF], True))
    b_line = jnp.stack(spread(mine[HALF:], False))
    a_line, b_line = lax.optimization_barrier((a_line, b_line))
    a_parts, b_parts = spread(a_line, False), spread(b_line, True)

    lines = (y + jnp.arange(SIDE, dtype=jnp.int32)) % SIDE
    other = 2 * lines + 1 - core
    own = 2 * lines + core
    swap = [(2 * i + c, 2 * i + 1 - c) for i in range(SIDE) for c in range(2)]

    def along(o):
        return [(2 * i + c, 2 * ((i + o) % SIDE) + c) for i in range(SIDE) for c in range(2)]

    def rest(capacity, a_parts, b_parts, r, stored, w_all):
        mixed = attend(
            capacity, set_lengths, live, row.reshape(1), offsets, token_ids, r, a_parts, b_parts
        )
        far = lax.ppermute(partials(other[2:3], mixed, w_all), "mp", swap)
        top, bottom = far_partials(own[2:3], mixed, w_all, far)
        from_below = lax.ppermute(top, "mp", along(1))
        from_above = lax.ppermute(bottom, "mp", along(3))
        order = jnp.array([1, 3, 0])
        got = lax.ppermute(partials(other[order], mixed, w_all), "mp", swap)
        mine = own[order]
        up, down = near_partials(mine, mixed, w_all, got, from_below, from_above)
        below = lax.ppermute(up, "mp", along(1))
        above = lax.ppermute(down, "mp", along(3))
        base = base_partial(mine, mixed, w_all, got)
        return finish(set_lengths, live, offsets, stored, base, below, above)

    which = jnp.sum(most > jnp.array(CAPACITIES[:-1]))
    branches = [lambda *args, c=c: rest(c, *args) for c in CAPACITIES]
    return lax.switch(which, branches, a_parts, b_parts, r, stored, w_all)


def solution(mesh):
    in_specs = (
        P("row", None),
        P("row"),
        P(),
        P(),
        P(),
        P(),
        P("row", "mp"),
        P("row", "mp"),
        P("row", "mp"),
        P("mp", "row"),
    )
    out_specs = P("row", None, "mp")
    return jax.shard_map(
        on_device, mesh=mesh, in_specs=in_specs, out_specs=out_specs, check_vma=False
    )
```

```python
import jax
import jax.numpy as jnp
from jax import lax
from jax.experimental import pallas as pl
from jax.experimental.pallas import tpu as pltpu
from jax.sharding import PartitionSpec as P

D = 5120
DH = 128
HEADS = 5
ROWS = 16
VOCAB = 512
SEQ = 128
SLOTS = 8
TABLE = VOCAB + SEQ
BLOCK = D // ROWS
FEATURES = 640
HALF = DH // 2
SIDE = 4
F32 = jnp.float32
BF16 = jnp.bfloat16
VMEM = 16 << 20
NOTE = 16
GROUP = 16
CAPACITIES = (640, 704, 768, 832, 896, SLOTS * SEQ)


def mm(a, b, dims):
    return lax.dot_general(a, b, (dims, ((), ())), preferred_element_type=F32)


def pack_kernel(place_ref, lens_ref, counts_ref, gain_ref, q_hbm, k_hbm, v_hbm, out_ref, info_ref, w_ref, turned_ref, sems):
    row = place_ref[0]
    copies = [
        pltpu.make_async_copy(source, w_ref.at[j], sems.at[j])
        for j, source in enumerate((q_hbm, k_hbm, v_hbm))
    ]
    for copy in copies:
        copy.start()
    live = counts_ref[row]
    total = jnp.int32(0)
    for s in range(SLOTS):
        info_ref[s] = GROUP * total
        groups = (lens_ref[s] + GROUP - 1) // GROUP
        total = total + jnp.where(s < live, groups, 0)
    info_ref[SLOTS] = live
    line = jnp.broadcast_to(gain_ref[pl.ds(row // 2, 1), :], (8, 2 * BLOCK))
    turned_ref[...] = line.T
    start = pl.multiple_of((row % 2) * BLOCK, 8)
    gain = turned_ref[pl.ds(start, BLOCK), :][:, :1]
    out_ref[ROWS - 1, :BLOCK] = jnp.zeros((BLOCK, DH), BF16)
    count = jnp.full((NOTE, DH), total, jnp.int32).astype(F32).astype(BF16)
    for i in range(ROWS):
        out_ref[i, BLOCK:] = count
    for j, copy in enumerate(copies):
        copy.wait()
        for h in range(HEADS):
            block = gain * w_ref[j, :, DH * h : DH * (h + 1)].astype(F32)
            out_ref[HEADS * j + h, :BLOCK] = block.astype(BF16)


def pack(place, lengths, counts, gain, w_query, w_key, w_value):
    stay = pl.BlockSpec(memory_space=pltpu.HBM)
    return pl.pallas_call(
        pack_kernel,
        grid_spec=pltpu.PrefetchScalarGridSpec(
            num_scalar_prefetch=3,
            grid=(1,),
            in_specs=[pl.BlockSpec((8, 2 * BLOCK), lambda i, *_: (0, 0)), stay, stay, stay],
            out_specs=[
                pl.BlockSpec((ROWS, BLOCK + NOTE, DH), lambda i, *_: (0, 0, 0)),
                pl.BlockSpec(memory_space=pltpu.SMEM),
            ],
            scratch_shapes=[
                pltpu.VMEM((3, BLOCK, FEATURES), BF16),
                pltpu.VMEM((2 * BLOCK, 8), F32),
                pltpu.SemaphoreType.DMA((3,)),
            ],
        ),
        out_shape=[
            jax.ShapeDtypeStruct((ROWS, BLOCK + NOTE, DH), BF16),
            jax.ShapeDtypeStruct((2 * SLOTS,), jnp.int32),
        ],
        compiler_params=pltpu.CompilerParams(vmem_limit_bytes=VMEM),
        name="pack",
    )(place, lengths, counts, gain, w_query, w_key, w_value)


def table_kernel(e_ref, p_ref, w_ref, t_ref, t_acc):
    step = pl.program_id(0)

    @pl.when(step == 0)
    def _():
        t_acc[...] = jnp.zeros_like(t_acc)

    w = w_ref[:, :BLOCK].reshape(2 * BLOCK, DH)
    t_acc[:, :VOCAB] += mm(w, e_ref[...], ((0,), (1,)))
    t_acc[:, VOCAB:] += mm(w, p_ref[...], ((0,), (1,)))

    @pl.when(step == pl.num_programs(0) - 1)
    def _():
        t_ref[...] = t_acc[...].astype(BF16)


def project_tables(embed_table, position_table, w_block):
    return pl.pallas_call(
        table_kernel,
        grid=(ROWS // 2,),
        in_specs=[
            pl.BlockSpec((VOCAB, 2 * BLOCK), lambda k: (0, k)),
            pl.BlockSpec((SEQ, 2 * BLOCK), lambda k: (0, k)),
            pl.BlockSpec((2, BLOCK + NOTE, DH), lambda k: (k, 0, 0)),
        ],
        out_specs=pl.BlockSpec((DH, TABLE), lambda k: (0, 0)),
        out_shape=jax.ShapeDtypeStruct((DH, TABLE), BF16),
        scratch_shapes=[pltpu.VMEM((DH, TABLE), F32)],
        compiler_params=pltpu.CompilerParams(vmem_limit_bytes=VMEM),
        name="project_tables",
    )(embed_table, position_table, w_block)


def scale_kernel(e_ref, p_ref, r_ref, g_acc, ee_acc, pp_acc):
    step = pl.program_id(0)

    @pl.when(step == 0)
    def _():
        g_acc[...] = jnp.zeros_like(g_acc)
        ee_acc[...] = jnp.zeros_like(ee_acc)
        pp_acc[...] = jnp.zeros_like(pp_acc)

    e, p = e_ref[...], p_ref[...]
    g_acc[...] += mm(e, p, ((1,), (1,)))
    pp_acc[...] += mm(p, p, ((1,), (1,)))
    wide = e.astype(F32)
    square = wide * wide
    folded = square[:, :128]
    for k in range(1, 2 * BLOCK // 128):
        folded += square[:, 128 * k : 128 * (k + 1)]
    ee_acc[...] += folded

    @pl.when(step == pl.num_programs(0) - 1)
    def _():
        ee = jnp.sum(ee_acc[...], axis=1, keepdims=True)
        diagonal = lax.broadcasted_iota(jnp.int32, (SEQ, SEQ), 0) == lax.broadcasted_iota(
            jnp.int32, (SEQ, SEQ), 1
        )
        pp = jnp.sum(jnp.where(diagonal, pp_acc[...], 0.0), axis=0, keepdims=True)
        total = jnp.maximum(ee + 2.0 * g_acc[...] + pp, 0.0)
        r_ref[...] = lax.rsqrt(total * (1.0 / D) + 1e-05)


def norm_scales(embed_table, position_table):
    return pl.pallas_call(
        scale_kernel,
        grid=(ROWS // 2,),
        in_specs=[
            pl.BlockSpec((VOCAB, 2 * BLOCK), lambda k: (0, k)),
            pl.BlockSpec((SEQ, 2 * BLOCK), lambda k: (0, k)),
        ],
        out_specs=pl.BlockSpec((VOCAB, SEQ), lambda k: (0, 0)),
        out_shape=jax.ShapeDtypeStruct((VOCAB, SEQ), F32),
        scratch_shapes=[
            pltpu.VMEM((VOCAB, SEQ), F32),
            pltpu.VMEM((VOCAB, 128), F32),
            pltpu.VMEM((SEQ, SEQ), F32),
        ],
        compiler_params=pltpu.CompilerParams(vmem_limit_bytes=VMEM),
        cost_estimate=pl.CostEstimate(flops=2 * TABLE * SEQ * D, transcendentals=VOCAB * SEQ, bytes_accessed=2 * TABLE * D),
        name="norm_scales",
    )(embed_table, position_table)


def residual_kernel(info_ref, place_ref, ids_ref, e_ref, p_ref, out_ref):
    slot = pl.program_id(0)

    @pl.when(slot < info_ref[SLOTS])
    def _():
        hit = lax.broadcasted_iota(jnp.int32, (VOCAB, SEQ), 0) == ids_ref[pl.ds(slot, 1), :]
        pick = jnp.where(hit, 1.0, 0.0).astype(BF16)
        stored = mm(pick, e_ref[...], ((0,), (0,))) + p_ref[...].astype(F32)
        out_ref[0] = stored.astype(BF16)

    @pl.when(slot >= info_ref[SLOTS])
    def _():
        out_ref[...] = jnp.zeros_like(out_ref)


def residual(info, place, ids, embed_table, position_table):
    return pl.pallas_call(
        residual_kernel,
        grid_spec=pltpu.PrefetchScalarGridSpec(
            num_scalar_prefetch=2,
            grid=(SLOTS,),
            in_specs=[
                pl.BlockSpec((SLOTS, SEQ), lambda s, *_: (0, 0)),
                pl.BlockSpec((VOCAB, FEATURES), lambda s, info, place: (0, place[1])),
                pl.BlockSpec((SEQ, FEATURES), lambda s, info, place: (0, place[1])),
            ],
            out_specs=pl.BlockSpec((1, SEQ, FEATURES), lambda s, *_: (s, 0, 0)),
        ),
        out_shape=jax.ShapeDtypeStruct((SLOTS, SEQ, FEATURES), BF16),
        compiler_params=pltpu.CompilerParams(vmem_limit_bytes=VMEM),
        cost_estimate=pl.CostEstimate(flops=2 * SLOTS * SEQ * VOCAB * FEATURES, transcendentals=0, bytes_accessed=4 * SLOTS * SEQ * FEATURES),
        name="residual",
    )(info, place, ids, embed_table, position_table)


def attend_kernel(lens_ref, info_ref, place_ref, ids_ref, r_ref, *refs):
    a_refs, b_refs = refs[:SIDE], refs[SIDE : 2 * SIDE]
    out_ref, table_ref, set_ref = refs[2 * SIDE :]
    step = pl.program_id(0)
    z, x = place_ref[0] // SIDE, place_ref[0] % SIDE

    @pl.when(step == 0)
    def _():
        for dz in range(SIDE):
            for dx in range(SIDE):
                source = SIDE * ((z + SIDE - dz) % SIDE) + (x + SIDE - dx) % SIDE
                table_ref[pl.ds(source, 1), :HALF] = a_refs[dz][dx : dx + 1]
                table_ref[pl.ds(source, 1), HALF:] = b_refs[dx][dz : dz + 1]
        out_ref[...] = jnp.zeros_like(out_ref)

    @pl.when(2 * step < info_ref[SLOTS])
    def _():
        vocab = lax.broadcasted_iota(jnp.int32, (VOCAB, SEQ), 0)
        eye = lax.broadcasted_iota(jnp.int32, (SEQ, SEQ), 0) == lax.broadcasted_iota(
            jnp.int32, (SEQ, SEQ), 1
        )
        picks, scales = [], []
        for s in range(2):
            hit = vocab == ids_ref[pl.ds(2 * step + s, 1), :]
            scales.append(jnp.sum(jnp.where(hit, r_ref[...], 0.0), axis=0, keepdims=True))
            picks.append(
                jnp.concatenate(
                    [jnp.where(hit, 1.0, 0.0).astype(BF16), jnp.where(eye, 1.0, 0.0).astype(BF16)], 0
                )
            )
        pick = jnp.concatenate(picks, axis=1)
        scale = jnp.concatenate(scales, axis=1)
        table = table_ref[: 3 * HEADS].reshape(3 * HEADS * DH, TABLE)
        rows = (mm(table, pick, ((1,), (0,))) * scale).astype(BF16)
        key_at = lax.broadcasted_iota(jnp.int32, (SEQ, SEQ), 0)
        for s in range(2):
            valid = key_at < lens_ref[2 * step + s]
            cols = slice(SEQ * s, SEQ * (s + 1))
            for h in range(HEADS):
                q = rows[DH * h : DH * (h + 1), cols]
                k = rows[DH * (HEADS + h) : DH * (HEADS + h + 1), cols]
                v = rows[DH * (2 * HEADS + h) : DH * (2 * HEADS + h + 1), cols]
                scores = mm(k, q, ((0,), (0,))) * DH ** (-0.5)
                scores = jnp.where(valid, scores, -1e30)
                expo = jnp.exp(scores - jnp.max(scores, axis=0, keepdims=True))
                weights = (expo / jnp.sum(expo, axis=0, keepdims=True)).astype(BF16)
                mixed = mm(v, weights, ((1,), (0,)))
                set_ref[s, :, DH * h : DH * (h + 1)] = mixed.T.astype(BF16)
        for s in range(2):
            for i in range(SEQ // GROUP):

                @pl.when((2 * step + s < info_ref[SLOTS]) & (GROUP * i < lens_ref[2 * step + s]))
                def _(s=s, i=i):
                    at = pl.multiple_of(info_ref[2 * step + s] + GROUP * i, GROUP)
                    out_ref[pl.ds(at, GROUP), :] = set_ref[s, GROUP * i : GROUP * (i + 1), :]


def attend(capacity, lengths, info, place, ids, r, a_parts, b_parts):
    quarter = pl.BlockSpec((SIDE, HALF, TABLE), lambda i, *_: (0, 0, 0))
    return pl.pallas_call(
        attend_kernel,
        grid_spec=pltpu.PrefetchScalarGridSpec(
            num_scalar_prefetch=3,
            grid=(SLOTS // 2,),
            in_specs=[
                pl.BlockSpec((SLOTS, SEQ), lambda i, *_: (0, 0)),
                pl.BlockSpec((VOCAB, SEQ), lambda i, *_: (0, 0)),
                *[quarter] * (2 * SIDE),
            ],
            out_specs=pl.BlockSpec((capacity, FEATURES), lambda i, *_: (0, 0)),
            scratch_shapes=[
                pltpu.VMEM((ROWS, DH, TABLE), BF16),
                pltpu.VMEM((2, SEQ, FEATURES), BF16),
            ],
        ),
        out_shape=jax.ShapeDtypeStruct((capacity, FEATURES), BF16),
        compiler_params=pltpu.CompilerParams(vmem_limit_bytes=VMEM),
        name="attend",
    )(lengths, info, place, ids, r, *a_parts, *b_parts)


def product(a_ref, other_ref, w_ref, w_other_ref):
    mine = mm(a_ref[...], w_ref[...].reshape(FEATURES, FEATURES), ((1,), (1,)))
    theirs = jnp.concatenate([w_other_ref[1], w_other_ref[0]], axis=0)
    return mine + mm(other_ref[...], theirs, ((1,), (1,)))


def pick(ahead):
    def block(place, core):
        return 2 * ((place[3] + ahead) % SIDE) + core

    shape = (2, BLOCK, FEATURES)
    return [
        pl.BlockSpec(shape, lambda i, place: (block(place, place[2]), 0, 0)),
        pl.BlockSpec(shape, lambda i, place: (block(place, 1 - place[2]), 0, 0)),
    ]


def far_kernel(place_ref, a_ref, other_ref, w_ref, w_other_ref, top_ref, bottom_ref):
    half = pl.program_id(0)
    total = product(a_ref, other_ref, w_ref, w_other_ref).astype(BF16)

    @pl.when(half == 0)
    def _():
        top_ref[...] = total

    @pl.when(half == 1)
    def _():
        bottom_ref[...] = total


def far_partials(place, mixed, other, w):
    tile = mixed.shape[0] // 2
    rows = pl.BlockSpec((tile, FEATURES), lambda i, place: (i, 0))
    whole = pl.BlockSpec((tile, FEATURES), lambda i, place: (0, 0))
    return pl.pallas_call(
        far_kernel,
        grid_spec=pltpu.PrefetchScalarGridSpec(
            num_scalar_prefetch=1,
            grid=(2,),
            in_specs=[rows, rows, *pick(2)],
            out_specs=[whole, whole],
        ),
        out_shape=[jax.ShapeDtypeStruct((tile, FEATURES), BF16)] * 2,
        compiler_params=pltpu.CompilerParams(vmem_limit_bytes=VMEM),
        name="far_partials",
    )(place, mixed, other, w, w)


def free_kernel(place_ref, a0, o0, a1, o1, w0, w1, w2, w3, up_ref, down_ref):
    up_ref[...] = product(a1, o1, w0, w1).astype(BF16)
    down_ref[...] = product(a0, o0, w2, w3).astype(BF16)


def free_partials(place, mixed, other, w):
    tile = mixed.shape[0] // 2
    first = pl.BlockSpec((tile, FEATURES), lambda i, place: (0, 0))
    second = pl.BlockSpec((tile, FEATURES), lambda i, place: (1, 0))
    return pl.pallas_call(
        free_kernel,
        grid_spec=pltpu.PrefetchScalarGridSpec(
            num_scalar_prefetch=1,
            grid=(1,),
            in_specs=[first, first, second, second, *pick(1), *pick(3)],
            out_specs=[first, first],
        ),
        out_shape=[jax.ShapeDtypeStruct((tile, FEATURES), BF16)] * 2,
        compiler_params=pltpu.CompilerParams(vmem_limit_bytes=VMEM),
        name="free_partials",
    )(place, mixed, other, mixed, other, w, w, w, w)


def relay_kernel(place_ref, a0, o0, a1, o1, w0, w1, w2, w3, from_below, from_above, up_ref, down_ref):
    up_ref[...] = (product(a0, o0, w0, w1) + from_below[...].astype(F32)).astype(BF16)
    down_ref[...] = (product(a1, o1, w2, w3) + from_above[...].astype(F32)).astype(BF16)


def relay_partials(place, mixed, other, w, from_below, from_above):
    tile = mixed.shape[0] // 2
    first = pl.BlockSpec((tile, FEATURES), lambda i, place: (0, 0))
    second = pl.BlockSpec((tile, FEATURES), lambda i, place: (1, 0))
    return pl.pallas_call(
        relay_kernel,
        grid_spec=pltpu.PrefetchScalarGridSpec(
            num_scalar_prefetch=1,
            grid=(1,),
            in_specs=[first, first, second, second, *pick(1), *pick(3), first, first],
            out_specs=[first, first],
        ),
        out_shape=[jax.ShapeDtypeStruct((tile, FEATURES), BF16)] * 2,
        compiler_params=pltpu.CompilerParams(vmem_limit_bytes=VMEM),
        name="relay_partials",
    )(place, mixed, other, mixed, other, w, w, w, w, from_below, from_above)


def base_kernel(place_ref, a_ref, other_ref, w_ref, w_other_ref, out_ref):
    out_ref[...] = product(a_ref, other_ref, w_ref, w_other_ref)


def base_partial(place, mixed, other, w):
    tokens = mixed.shape[0]
    rows = pl.BlockSpec((tokens // 2, FEATURES), lambda i, place: (i, 0))
    return pl.pallas_call(
        base_kernel,
        grid_spec=pltpu.PrefetchScalarGridSpec(
            num_scalar_prefetch=1,
            grid=(2,),
            in_specs=[rows, rows, *pick(0)],
            out_specs=rows,
        ),
        out_shape=jax.ShapeDtypeStruct((tokens, FEATURES), F32),
        compiler_params=pltpu.CompilerParams(vmem_limit_bytes=VMEM),
        name="base_partial",
    )(place, mixed, other, w, w)


def finish_kernel(lens_ref, info_ref, stored_ref, base_ref, *refs):
    below, above, out_ref = refs[:2], refs[2:4], refs[4]
    slot = pl.program_id(0)
    tile = below[0].shape[0]
    for i in range(SEQ // GROUP):
        here = slice(GROUP * i, GROUP * (i + 1))
        live = (slot < info_ref[SLOTS]) & (GROUP * i < lens_ref[slot])
        start = pl.multiple_of(info_ref[slot] + GROUP * i, GROUP)
        for half in range(2):

            @pl.when(live & ((start >= tile) if half else (start < tile)))
            def _(i=i, here=here, half=half, start=start):
                at = pl.ds(pl.multiple_of(start - half * tile, GROUP), GROUP)
                total = base_ref[pl.ds(start, GROUP), :] + below[half][at, :].astype(F32)
                total += above[half][at, :].astype(F32)
                place = GROUP * i + lax.broadcasted_iota(jnp.int32, (GROUP, FEATURES), 0)
                result = stored_ref[0, here].astype(F32) + total
                out_ref[0, here] = jnp.where(place < lens_ref[slot], result, 0.0).astype(BF16)

        @pl.when(jnp.logical_not(live))
        def _(here=here):
            out_ref[0, here] = jnp.zeros((GROUP, FEATURES), BF16)


def finish(lengths, info, stored, base, below, above):
    whole = pl.BlockSpec(base.shape, lambda s, *_: (0, 0))
    half = pl.BlockSpec(below[0].shape, lambda s, *_: (0, 0))
    one = pl.BlockSpec((1, SEQ, FEATURES), lambda s, *_: (s, 0, 0))
    return pl.pallas_call(
        finish_kernel,
        grid_spec=pltpu.PrefetchScalarGridSpec(
            num_scalar_prefetch=2,
            grid=(SLOTS,),
            in_specs=[one, whole, half, half, half, half],
            out_specs=one,
        ),
        out_shape=jax.ShapeDtypeStruct((SLOTS, SEQ, FEATURES), BF16),
        compiler_params=pltpu.CompilerParams(vmem_limit_bytes=VMEM),
        name="finish",
    )(lengths, info, stored, base, *below, *above)


def on_device(
    token_ids,
    set_lengths,
    live_counts,
    embed_table,
    position_table,
    norm_gain,
    w_query,
    w_key,
    w_value,
    w_out,
):
    row = lax.axis_index("row")
    part = lax.axis_index("mp")
    y, core = part // 2, part % 2
    place = jnp.stack([row, part, core, y])

    def shifted(o, along_x):
        pairs = []
        for z in range(SIDE):
            for x in range(SIDE):
                to = SIDE * z + (x + o) % SIDE if along_x else SIDE * ((z + o) % SIDE) + x
                pairs.append((SIDE * z + x, to))
        return pairs

    def spread(value, along_x):
        near = {o: lax.ppermute(value, "row", shifted(o, along_x)) for o in (1, 3, 2)}
        return [value, near[1], near[2], near[3]]

    turned = w_out.T
    cross = []
    for z in range(SIDE):
        for x in range(SIDE):
            for line in range(SIDE):
                c = 1 - x // 2
                source = (SIDE * z + x) * 8 + 2 * line + c
                cross.append((source, (SIDE * z + 3 - x) * 8 + 2 * line + 1 - c))
    crossed = lax.ppermute(turned, ("row", "mp"), cross)
    tiles = jnp.where((row % SIDE) // 2 == core, turned, crossed)

    packed, info = pack(
        place, set_lengths, live_counts, norm_gain.reshape(8, 2 * BLOCK), w_query, w_key, w_value
    )
    w_block = lax.all_to_all(packed, "row", 0, 0)
    w_block, tiles = lax.optimization_barrier((w_block, tiles))
    w_all = lax.all_gather(tiles, "row", axis=0)
    most = GROUP * jnp.max(w_block[:, BLOCK, 0].astype(F32)).astype(jnp.int32)
    mine = project_tables(embed_table, position_table, w_block)

    a_line = jnp.stack(spread(mine[:HALF], True))
    b_line = jnp.stack(spread(mine[HALF:], False))
    a_line, b_line = lax.optimization_barrier((a_line, b_line))
    a_parts, b_parts = spread(a_line, False), spread(b_line, True)
    embed_late, a_parts[1] = lax.optimization_barrier((embed_table, a_parts[1]))
    r = norm_scales(embed_late, position_table)

    swap = [(2 * i + c, 2 * i + 1 - c) for i in range(SIDE) for c in range(2)]

    def along(o):
        return [(2 * i + c, 2 * ((i + o) % SIDE) + c) for i in range(SIDE) for c in range(2)]

    def rest(capacity, a_parts, b_parts, w, r):
        mixed = attend(capacity, set_lengths, info, place, token_ids, r, a_parts, b_parts)
        other = lax.ppermute(mixed, "mp", swap)
        top, bottom = far_partials(place, mixed, other, w)
        from_below = lax.ppermute(top, "mp", along(1))
        from_above = lax.ppermute(bottom, "mp", along(3))
        free_up, free_down = free_partials(place, mixed, other, w)
        below_low = lax.ppermute(free_up, "mp", along(1))
        above_high = lax.ppermute(free_down, "mp", along(3))
        up, down = relay_partials(place, mixed, other, w, from_below, from_above)
        below_high = lax.ppermute(up, "mp", along(1))
        above_low = lax.ppermute(down, "mp", along(3))
        base = base_partial(place, mixed, other, w)
        stored = residual(info, place, token_ids, embed_table, position_table)
        return finish(
            set_lengths, info, stored, base, (below_high, below_low), (above_high, above_low)
        )

    return rest(SLOTS * SEQ, a_parts, b_parts, w_all, r)


def solution(mesh):
    in_specs = (
        P("row", None),
        P("row"),
        P(),
        P(),
        P(),
        P(),
        P("row", "mp"),
        P("row", "mp"),
        P("row", "mp"),
        P("mp", "row"),
    )
    out_specs = P("row", None, "mp")
    return jax.shard_map(
        on_device, mesh=mesh, in_specs=in_specs, out_specs=out_specs, check_vma=False
    )
```

```python
import jax
import jax.numpy as jnp
from jax import lax
from jax.experimental import pallas as pl
from jax.experimental.pallas import tpu as pltpu
from jax.sharding import PartitionSpec as P

D = 5120
DH = 128
HEADS = 5
ROWS = 16
VOCAB = 512
SEQ = 128
SLOTS = 8
TABLE = VOCAB + SEQ
BLOCK = D // ROWS
FEATURES = 640
HALF = DH // 2
SIDE = 4
F32 = jnp.float32
BF16 = jnp.bfloat16
VMEM = 16 << 20
MOST = 57 << 20
GROUP = 16


def mm(a, b, dims):
    return lax.dot_general(a, b, (dims, ((), ())), preferred_element_type=F32)


def pack_kernel(place_ref, lens_ref, counts_ref, gain_ref, q_hbm, k_hbm, v_hbm, out_ref, info_ref, w_ref, turned_ref, sems):
    row = place_ref[0]
    copies = [
        pltpu.make_async_copy(source, w_ref.at[j], sems.at[j])
        for j, source in enumerate((q_hbm, k_hbm, v_hbm))
    ]
    for copy in copies:
        copy.start()
    live = counts_ref[row]
    total = jnp.int32(0)
    for s in range(SLOTS):
        info_ref[s] = GROUP * total
        groups = (lens_ref[s] + GROUP - 1) // GROUP
        total = total + jnp.where(s < live, groups, 0)
    info_ref[SLOTS] = live
    line = jnp.broadcast_to(gain_ref[pl.ds(row // 2, 1), :], (8, 2 * BLOCK))
    turned_ref[...] = line.T
    start = pl.multiple_of((row % 2) * BLOCK, 8)
    gain = turned_ref[pl.ds(start, BLOCK), :][:, :1]
    out_ref[ROWS - 1] = jnp.zeros((BLOCK, DH), BF16)
    for j, copy in enumerate(copies):
        copy.wait()
        for h in range(HEADS):
            block = gain * w_ref[j, :, DH * h : DH * (h + 1)].astype(F32)
            out_ref[HEADS * j + h] = block.astype(BF16)


def pack(place, lengths, counts, gain, w_query, w_key, w_value):
    stay = pl.BlockSpec(memory_space=pltpu.HBM)
    return pl.pallas_call(
        pack_kernel,
        grid_spec=pltpu.PrefetchScalarGridSpec(
            num_scalar_prefetch=3,
            grid=(1,),
            in_specs=[pl.BlockSpec((8, 2 * BLOCK), lambda i, *_: (0, 0)), stay, stay, stay],
            out_specs=[
                pl.BlockSpec((ROWS, BLOCK, DH), lambda i, *_: (0, 0, 0)),
                pl.BlockSpec(memory_space=pltpu.SMEM),
            ],
            scratch_shapes=[
                pltpu.VMEM((3, BLOCK, FEATURES), BF16),
                pltpu.VMEM((2 * BLOCK, 8), F32),
                pltpu.SemaphoreType.DMA((3,)),
            ],
        ),
        out_shape=[
            jax.ShapeDtypeStruct((ROWS, BLOCK, DH), BF16),
            jax.ShapeDtypeStruct((2 * SLOTS,), jnp.int32),
        ],
        compiler_params=pltpu.CompilerParams(vmem_limit_bytes=MOST),
        name="pack",
    )(place, lengths, counts, gain, w_query, w_key, w_value)


def table_kernel(e_ref, p_ref, w_ref, t_ref, t_acc):
    step = pl.program_id(0)

    @pl.when(step == 0)
    def _():
        t_acc[...] = jnp.zeros_like(t_acc)

    w = w_ref[...].reshape(2 * BLOCK, DH)
    t_acc[:, :VOCAB] += mm(w, e_ref[...], ((0,), (1,)))
    t_acc[:, VOCAB:] += mm(w, p_ref[...], ((0,), (1,)))

    @pl.when(step == pl.num_programs(0) - 1)
    def _():
        t_ref[...] = t_acc[...].astype(BF16)


def project_tables(embed_table, position_table, w_block):
    return pl.pallas_call(
        table_kernel,
        grid=(ROWS // 2,),
        in_specs=[
            pl.BlockSpec((VOCAB, 2 * BLOCK), lambda k: (0, k)),
            pl.BlockSpec((SEQ, 2 * BLOCK), lambda k: (0, k)),
            pl.BlockSpec((2, BLOCK, DH), lambda k: (k, 0, 0)),
        ],
        out_specs=pl.BlockSpec((DH, TABLE), lambda k: (0, 0)),
        out_shape=jax.ShapeDtypeStruct((DH, TABLE), BF16),
        scratch_shapes=[pltpu.VMEM((DH, TABLE), F32)],
        compiler_params=pltpu.CompilerParams(vmem_limit_bytes=VMEM),
        name="project_tables",
    )(embed_table, position_table, w_block)


def scale_kernel(e_ref, p_ref, r_ref, g_acc, ee_acc, pp_acc):
    step = pl.program_id(0)

    @pl.when(step == 0)
    def _():
        g_acc[...] = jnp.zeros_like(g_acc)
        ee_acc[...] = jnp.zeros_like(ee_acc)
        pp_acc[...] = jnp.zeros_like(pp_acc)

    e, p = e_ref[...], p_ref[...]
    g_acc[...] += mm(e, p, ((1,), (1,)))
    pp_acc[...] += mm(p, p, ((1,), (1,)))
    wide = e.astype(F32)
    square = wide * wide
    folded = square[:, :128]
    for k in range(1, 2 * BLOCK // 128):
        folded += square[:, 128 * k : 128 * (k + 1)]
    ee_acc[...] += folded

    @pl.when(step == pl.num_programs(0) - 1)
    def _():
        ee = jnp.sum(ee_acc[...], axis=1, keepdims=True)
        diagonal = lax.broadcasted_iota(jnp.int32, (SEQ, SEQ), 0) == lax.broadcasted_iota(
            jnp.int32, (SEQ, SEQ), 1
        )
        pp = jnp.sum(jnp.where(diagonal, pp_acc[...], 0.0), axis=0, keepdims=True)
        total = jnp.maximum(ee + 2.0 * g_acc[...] + pp, 0.0)
        r_ref[...] = lax.rsqrt(total * (1.0 / D) + 1e-05)


def norm_scales(embed_table, position_table):
    return pl.pallas_call(
        scale_kernel,
        grid=(ROWS // 2,),
        in_specs=[
            pl.BlockSpec((VOCAB, 2 * BLOCK), lambda k: (0, k)),
            pl.BlockSpec((SEQ, 2 * BLOCK), lambda k: (0, k)),
        ],
        out_specs=pl.BlockSpec((VOCAB, SEQ), lambda k: (0, 0)),
        out_shape=jax.ShapeDtypeStruct((VOCAB, SEQ), F32),
        scratch_shapes=[
            pltpu.VMEM((VOCAB, SEQ), F32),
            pltpu.VMEM((VOCAB, 128), F32),
            pltpu.VMEM((SEQ, SEQ), F32),
        ],
        compiler_params=pltpu.CompilerParams(vmem_limit_bytes=VMEM),
        cost_estimate=pl.CostEstimate(flops=2 * TABLE * SEQ * D, transcendentals=VOCAB * SEQ, bytes_accessed=2 * TABLE * D),
        name="norm_scales",
    )(embed_table, position_table)


def residual_kernel(info_ref, place_ref, ids_ref, e_ref, p_ref, out_ref):
    slot = pl.program_id(0)

    @pl.when(slot < info_ref[SLOTS])
    def _():
        hit = lax.broadcasted_iota(jnp.int32, (VOCAB, SEQ), 0) == ids_ref[pl.ds(slot, 1), :]
        pick = jnp.where(hit, 1.0, 0.0).astype(BF16)
        stored = mm(pick, e_ref[...], ((0,), (0,))) + p_ref[...].astype(F32)
        out_ref[0] = stored.astype(BF16)

    @pl.when(slot >= info_ref[SLOTS])
    def _():
        out_ref[...] = jnp.zeros_like(out_ref)


def residual(info, place, ids, embed_table, position_table):
    return pl.pallas_call(
        residual_kernel,
        grid_spec=pltpu.PrefetchScalarGridSpec(
            num_scalar_prefetch=2,
            grid=(SLOTS,),
            in_specs=[
                pl.BlockSpec((SLOTS, SEQ), lambda s, *_: (0, 0)),
                pl.BlockSpec((VOCAB, FEATURES), lambda s, info, place: (0, place[1])),
                pl.BlockSpec((SEQ, FEATURES), lambda s, info, place: (0, place[1])),
            ],
            out_specs=pl.BlockSpec((1, SEQ, FEATURES), lambda s, *_: (s, 0, 0)),
        ),
        out_shape=jax.ShapeDtypeStruct((SLOTS, SEQ, FEATURES), BF16),
        compiler_params=pltpu.CompilerParams(vmem_limit_bytes=VMEM),
        cost_estimate=pl.CostEstimate(flops=2 * SLOTS * SEQ * VOCAB * FEATURES, transcendentals=0, bytes_accessed=4 * SLOTS * SEQ * FEATURES),
        name="residual",
    )(info, place, ids, embed_table, position_table)


def attend_kernel(lens_ref, info_ref, place_ref, ids_ref, r_ref, *refs):
    a_refs, b_refs = refs[:SIDE], refs[SIDE : 2 * SIDE]
    out_ref, table_ref, set_ref = refs[2 * SIDE :]
    step = pl.program_id(0)
    z, x = place_ref[0] // SIDE, place_ref[0] % SIDE

    @pl.when(step == 0)
    def _():
        for dz in range(SIDE):
            for dx in range(SIDE):
                source = SIDE * ((z + SIDE - dz) % SIDE) + (x + SIDE - dx) % SIDE
                table_ref[pl.ds(source, 1), :HALF] = a_refs[dz][dx : dx + 1]
                table_ref[pl.ds(source, 1), HALF:] = b_refs[dx][dz : dz + 1]
        out_ref[...] = jnp.zeros_like(out_ref)

    @pl.when(2 * step < info_ref[SLOTS])
    def _():
        vocab = lax.broadcasted_iota(jnp.int32, (VOCAB, SEQ), 0)
        eye = lax.broadcasted_iota(jnp.int32, (SEQ, SEQ), 0) == lax.broadcasted_iota(
            jnp.int32, (SEQ, SEQ), 1
        )
        picks, scales = [], []
        for s in range(2):
            hit = vocab == ids_ref[pl.ds(2 * step + s, 1), :]
            scales.append(jnp.sum(jnp.where(hit, r_ref[...], 0.0), axis=0, keepdims=True))
            picks.append(
                jnp.concatenate(
                    [jnp.where(hit, 1.0, 0.0).astype(BF16), jnp.where(eye, 1.0, 0.0).astype(BF16)], 0
                )
            )
        pick = jnp.concatenate(picks, axis=1)
        scale = jnp.concatenate(scales, axis=1)
        table = table_ref[: 3 * HEADS].reshape(3 * HEADS * DH, TABLE)
        rows = (mm(table, pick, ((1,), (0,))) * scale).astype(BF16)
        key_at = lax.broadcasted_iota(jnp.int32, (SEQ, SEQ), 0)
        for s in range(2):
            valid = key_at < lens_ref[2 * step + s]
            cols = slice(SEQ * s, SEQ * (s + 1))
            for h in range(HEADS):
                q = rows[DH * h : DH * (h + 1), cols]
                k = rows[DH * (HEADS + h) : DH * (HEADS + h + 1), cols]
                v = rows[DH * (2 * HEADS + h) : DH * (2 * HEADS + h + 1), cols]
                scores = mm(k, q, ((0,), (0,))) * DH ** (-0.5)
                scores = jnp.where(valid, scores, -1e30)
                expo = jnp.exp(scores - jnp.max(scores, axis=0, keepdims=True))
                weights = (expo / jnp.sum(expo, axis=0, keepdims=True)).astype(BF16)
                mixed = mm(v, weights, ((1,), (0,)))
                set_ref[s, :, DH * h : DH * (h + 1)] = mixed.T.astype(BF16)
        for s in range(2):
            for i in range(SEQ // GROUP):

                @pl.when((2 * step + s < info_ref[SLOTS]) & (GROUP * i < lens_ref[2 * step + s]))
                def _(s=s, i=i):
                    at = pl.multiple_of(info_ref[2 * step + s] + GROUP * i, GROUP)
                    out_ref[pl.ds(at, GROUP), :] = set_ref[s, GROUP * i : GROUP * (i + 1), :]


def attend(capacity, lengths, info, place, ids, r, a_parts, b_parts):
    quarter = pl.BlockSpec((SIDE, HALF, TABLE), lambda i, *_: (0, 0, 0))
    return pl.pallas_call(
        attend_kernel,
        grid_spec=pltpu.PrefetchScalarGridSpec(
            num_scalar_prefetch=3,
            grid=(SLOTS // 2,),
            in_specs=[
                pl.BlockSpec((SLOTS, SEQ), lambda i, *_: (0, 0)),
                pl.BlockSpec((VOCAB, SEQ), lambda i, *_: (0, 0)),
                *[quarter] * (2 * SIDE),
            ],
            out_specs=pl.BlockSpec((capacity, FEATURES), lambda i, *_: (0, 0)),
            scratch_shapes=[
                pltpu.VMEM((ROWS, DH, TABLE), BF16),
                pltpu.VMEM((2, SEQ, FEATURES), BF16),
            ],
        ),
        out_shape=jax.ShapeDtypeStruct((capacity, FEATURES), BF16),
        compiler_params=pltpu.CompilerParams(vmem_limit_bytes=VMEM),
        name="attend",
    )(lengths, info, place, ids, r, *a_parts, *b_parts)


def product(a_ref, other_ref, w_ref, w_other_ref):
    mine = mm(a_ref[...], w_ref[...].reshape(FEATURES, FEATURES), ((1,), (1,)))
    theirs = jnp.concatenate([w_other_ref[1], w_other_ref[0]], axis=0)
    return mine + mm(other_ref[...], theirs, ((1,), (1,)))


def pick(ahead):
    def block(place, core):
        return 2 * ((place[3] + ahead) % SIDE) + core

    shape = (2, BLOCK, FEATURES)
    return [
        pl.BlockSpec(shape, lambda i, place: (block(place, place[2]), 0, 0)),
        pl.BlockSpec(shape, lambda i, place: (block(place, 1 - place[2]), 0, 0)),
    ]


def far_kernel(place_ref, a_ref, other_ref, w_ref, w_other_ref, top_ref, bottom_ref):
    half = pl.program_id(0)
    total = product(a_ref, other_ref, w_ref, w_other_ref).astype(BF16)

    @pl.when(half == 0)
    def _():
        top_ref[...] = total

    @pl.when(half == 1)
    def _():
        bottom_ref[...] = total


def far_partials(place, mixed, other, w):
    tile = mixed.shape[0] // 2
    rows = pl.BlockSpec((tile, FEATURES), lambda i, place: (i, 0))
    whole = pl.BlockSpec((tile, FEATURES), lambda i, place: (0, 0))
    return pl.pallas_call(
        far_kernel,
        grid_spec=pltpu.PrefetchScalarGridSpec(
            num_scalar_prefetch=1,
            grid=(2,),
            in_specs=[rows, rows, *pick(2)],
            out_specs=[whole, whole],
        ),
        out_shape=[jax.ShapeDtypeStruct((tile, FEATURES), BF16)] * 2,
        compiler_params=pltpu.CompilerParams(vmem_limit_bytes=VMEM),
        name="far_partials",
    )(place, mixed, other, w, w)


def free_kernel(place_ref, a0, o0, a1, o1, w0, w1, w2, w3, up_ref, down_ref):
    up_ref[...] = product(a1, o1, w0, w1).astype(BF16)
    down_ref[...] = product(a0, o0, w2, w3).astype(BF16)


def free_partials(place, mixed, other, w):
    tile = mixed.shape[0] // 2
    first = pl.BlockSpec((tile, FEATURES), lambda i, place: (0, 0))
    second = pl.BlockSpec((tile, FEATURES), lambda i, place: (1, 0))
    return pl.pallas_call(
        free_kernel,
        grid_spec=pltpu.PrefetchScalarGridSpec(
            num_scalar_prefetch=1,
            grid=(1,),
            in_specs=[first, first, second, second, *pick(1), *pick(3)],
            out_specs=[first, first],
        ),
        out_shape=[jax.ShapeDtypeStruct((tile, FEATURES), BF16)] * 2,
        compiler_params=pltpu.CompilerParams(vmem_limit_bytes=VMEM),
        name="free_partials",
    )(place, mixed, other, mixed, other, w, w, w, w)


def relay_kernel(place_ref, a0, o0, a1, o1, w0, w1, w2, w3, from_below, from_above, up_ref, down_ref):
    up_ref[...] = (product(a0, o0, w0, w1) + from_below[...].astype(F32)).astype(BF16)
    down_ref[...] = (product(a1, o1, w2, w3) + from_above[...].astype(F32)).astype(BF16)


def relay_partials(place, mixed, other, w, from_below, from_above):
    tile = mixed.shape[0] // 2
    first = pl.BlockSpec((tile, FEATURES), lambda i, place: (0, 0))
    second = pl.BlockSpec((tile, FEATURES), lambda i, place: (1, 0))
    return pl.pallas_call(
        relay_kernel,
        grid_spec=pltpu.PrefetchScalarGridSpec(
            num_scalar_prefetch=1,
            grid=(1,),
            in_specs=[first, first, second, second, *pick(1), *pick(3), first, first],
            out_specs=[first, first],
        ),
        out_shape=[jax.ShapeDtypeStruct((tile, FEATURES), BF16)] * 2,
        compiler_params=pltpu.CompilerParams(vmem_limit_bytes=VMEM),
        name="relay_partials",
    )(place, mixed, other, mixed, other, w, w, w, w, from_below, from_above)


def base_kernel(place_ref, a_ref, other_ref, w_ref, w_other_ref, out_ref):
    out_ref[...] = product(a_ref, other_ref, w_ref, w_other_ref)


def base_partial(place, mixed, other, w):
    tokens = mixed.shape[0]
    rows = pl.BlockSpec((tokens // 2, FEATURES), lambda i, place: (i, 0))
    return pl.pallas_call(
        base_kernel,
        grid_spec=pltpu.PrefetchScalarGridSpec(
            num_scalar_prefetch=1,
            grid=(2,),
            in_specs=[rows, rows, *pick(0)],
            out_specs=rows,
        ),
        out_shape=jax.ShapeDtypeStruct((tokens, FEATURES), F32),
        compiler_params=pltpu.CompilerParams(vmem_limit_bytes=VMEM),
        name="base_partial",
    )(place, mixed, other, w, w)


def finish_kernel(lens_ref, info_ref, stored_ref, base_ref, *refs):
    below, above, out_ref = refs[:2], refs[2:4], refs[4]
    slot = pl.program_id(0)
    tile = below[0].shape[0]
    for i in range(SEQ // GROUP):
        here = slice(GROUP * i, GROUP * (i + 1))
        live = (slot < info_ref[SLOTS]) & (GROUP * i < lens_ref[slot])
        start = pl.multiple_of(info_ref[slot] + GROUP * i, GROUP)
        for half in range(2):

            @pl.when(live & ((start >= tile) if half else (start < tile)))
            def _(i=i, here=here, half=half, start=start):
                at = pl.ds(pl.multiple_of(start - half * tile, GROUP), GROUP)
                total = base_ref[pl.ds(start, GROUP), :] + below[half][at, :].astype(F32)
                total += above[half][at, :].astype(F32)
                place = GROUP * i + lax.broadcasted_iota(jnp.int32, (GROUP, FEATURES), 0)
                result = stored_ref[0, here].astype(F32) + total
                out_ref[0, here] = jnp.where(place < lens_ref[slot], result, 0.0).astype(BF16)

        @pl.when(jnp.logical_not(live))
        def _(here=here):
            out_ref[0, here] = jnp.zeros((GROUP, FEATURES), BF16)


def finish(lengths, info, stored, base, below, above):
    whole = pl.BlockSpec(base.shape, lambda s, *_: (0, 0))
    half = pl.BlockSpec(below[0].shape, lambda s, *_: (0, 0))
    one = pl.BlockSpec((1, SEQ, FEATURES), lambda s, *_: (s, 0, 0))
    return pl.pallas_call(
        finish_kernel,
        grid_spec=pltpu.PrefetchScalarGridSpec(
            num_scalar_prefetch=2,
            grid=(SLOTS,),
            in_specs=[one, whole, half, half, half, half],
            out_specs=one,
        ),
        out_shape=jax.ShapeDtypeStruct((SLOTS, SEQ, FEATURES), BF16),
        compiler_params=pltpu.CompilerParams(vmem_limit_bytes=VMEM),
        name="finish",
    )(lengths, info, stored, base, *below, *above)


def on_device(
    token_ids,
    set_lengths,
    live_counts,
    embed_table,
    position_table,
    norm_gain,
    w_query,
    w_key,
    w_value,
    w_out,
):
    row = lax.axis_index("row")
    part = lax.axis_index("mp")
    y, core = part // 2, part % 2
    place = jnp.stack([row, part, core, y])

    def shifted(o, along_x):
        pairs = []
        for z in range(SIDE):
            for x in range(SIDE):
                to = SIDE * z + (x + o) % SIDE if along_x else SIDE * ((z + o) % SIDE) + x
                pairs.append((SIDE * z + x, to))
        return pairs

    def spread(value, along_x):
        near = {o: lax.ppermute(value, "row", shifted(o, along_x)) for o in (1, 3, 2)}
        return [value, near[1], near[2], near[3]]

    packed, info = pack(
        place, set_lengths, live_counts, norm_gain.reshape(8, 2 * BLOCK), w_query, w_key, w_value
    )
    packed, w_out, embed_late = lax.optimization_barrier((packed, w_out, embed_table))
    turned = w_out.T
    cross = []
    for z in range(SIDE):
        for x in range(SIDE):
            for line in range(SIDE):
                c = 1 - x // 2
                source = (SIDE * z + x) * 8 + 2 * line + c
                cross.append((source, (SIDE * z + 3 - x) * 8 + 2 * line + 1 - c))
    crossed = lax.ppermute(turned, ("row", "mp"), cross)
    tiles = jnp.where((row % SIDE) // 2 == core, turned, crossed)
    r = norm_scales(embed_late, position_table)
    w_block = lax.all_to_all(packed, "row", 0, 0)
    w_block, tiles, r = lax.optimization_barrier((w_block, tiles, r))
    w_all = lax.all_gather(tiles, "row", axis=0)
    mine = project_tables(embed_table, position_table, w_block)

    a_line = jnp.stack(spread(mine[:HALF], True))
    b_line = jnp.stack(spread(mine[HALF:], False))
    a_line, b_line = lax.optimization_barrier((a_line, b_line))
    a_parts, b_parts = spread(a_line, False), spread(b_line, True)
    ids_late, a_parts[1] = lax.optimization_barrier((token_ids, a_parts[1]))
    stored = residual(info, place, ids_late, embed_table, position_table)
    swap = [(2 * i + c, 2 * i + 1 - c) for i in range(SIDE) for c in range(2)]

    def along(o):
        return [(2 * i + c, 2 * ((i + o) % SIDE) + c) for i in range(SIDE) for c in range(2)]

    def rest(capacity, a_parts, b_parts, w, r):
        mixed = attend(capacity, set_lengths, info, place, token_ids, r, a_parts, b_parts)
        other = lax.ppermute(mixed, "mp", swap)
        top, bottom = far_partials(place, mixed, other, w)
        from_below = lax.ppermute(top, "mp", along(1))
        from_above = lax.ppermute(bottom, "mp", along(3))
        free_up, free_down = free_partials(place, mixed, other, w)
        below_low = lax.ppermute(free_up, "mp", along(1))
        above_high = lax.ppermute(free_down, "mp", along(3))
        up, down = relay_partials(place, mixed, other, w, from_below, from_above)
        below_high = lax.ppermute(up, "mp", along(1))
        above_low = lax.ppermute(down, "mp", along(3))
        base = base_partial(place, mixed, other, w)
        return finish(
            set_lengths, info, stored, base, (below_high, below_low), (above_high, above_low)
        )

    return rest(SLOTS * SEQ, a_parts, b_parts, w_all, r)


def solution(mesh):
    in_specs = (
        P("row", None),
        P("row"),
        P(),
        P(),
        P(),
        P(),
        P("row", "mp"),
        P("row", "mp"),
        P("row", "mp"),
        P("mp", "row"),
    )
    out_specs = P("row", None, "mp")
    return jax.shard_map(
        on_device, mesh=mesh, in_specs=in_specs, out_specs=out_specs, check_vma=False
    )
```

```python
import jax
import jax.numpy as jnp
from jax import lax
from jax.experimental import pallas as pl
from jax.experimental.pallas import tpu as pltpu
from jax.sharding import PartitionSpec as P

D = 5120
DH = 128
HEADS = 5
ROWS = 16
VOCAB = 512
SEQ = 128
SLOTS = 8
TABLE = VOCAB + SEQ
BLOCK = D // ROWS
FEATURES = 640
HALF = DH // 2
SIDE = 4
F32 = jnp.float32
BF16 = jnp.bfloat16
VMEM = 16 << 20
MOST = 57 << 20
GROUP = 16


def mm(a, b, dims):
    return lax.dot_general(a, b, (dims, ((), ())), preferred_element_type=F32)


def pack_kernel(place_ref, lens_ref, counts_ref, gain_ref, q_hbm, k_hbm, v_hbm, out_ref, info_ref, w_ref, turned_ref, sems):
    row = place_ref[0]
    copies = [
        pltpu.make_async_copy(source, w_ref.at[j], sems.at[j])
        for j, source in enumerate((q_hbm, k_hbm, v_hbm))
    ]
    for copy in copies:
        copy.start()
    live = counts_ref[row]
    total = jnp.int32(0)
    for s in range(SLOTS):
        info_ref[s] = GROUP * total
        groups = (lens_ref[s] + GROUP - 1) // GROUP
        total = total + jnp.where(s < live, groups, 0)
    info_ref[SLOTS] = live
    line = jnp.broadcast_to(gain_ref[pl.ds(row // 2, 1), :], (8, 2 * BLOCK))
    turned_ref[...] = line.T
    start = pl.multiple_of((row % 2) * BLOCK, 8)
    gain = turned_ref[pl.ds(start, BLOCK), :][:, :1]
    out_ref[ROWS - 1] = jnp.zeros((BLOCK, DH), BF16)
    for j, copy in enumerate(copies):
        copy.wait()
        for h in range(HEADS):
            block = gain * w_ref[j, :, DH * h : DH * (h + 1)].astype(F32)
            out_ref[HEADS * j + h] = block.astype(BF16)


def pack(place, lengths, counts, gain, w_query, w_key, w_value):
    stay = pl.BlockSpec(memory_space=pltpu.HBM)
    return pl.pallas_call(
        pack_kernel,
        grid_spec=pltpu.PrefetchScalarGridSpec(
            num_scalar_prefetch=3,
            grid=(1,),
            in_specs=[pl.BlockSpec((8, 2 * BLOCK), lambda i, *_: (0, 0)), stay, stay, stay],
            out_specs=[
                pl.BlockSpec((ROWS, BLOCK, DH), lambda i, *_: (0, 0, 0)),
                pl.BlockSpec(memory_space=pltpu.SMEM),
            ],
            scratch_shapes=[
                pltpu.VMEM((3, BLOCK, FEATURES), BF16),
                pltpu.VMEM((2 * BLOCK, 8), F32),
                pltpu.SemaphoreType.DMA((3,)),
            ],
        ),
        out_shape=[
            jax.ShapeDtypeStruct((ROWS, BLOCK, DH), BF16),
            jax.ShapeDtypeStruct((2 * SLOTS,), jnp.int32),
        ],
        compiler_params=pltpu.CompilerParams(vmem_limit_bytes=MOST),
        name="pack",
    )(place, lengths, counts, gain, w_query, w_key, w_value)


def table_kernel(e_ref, p_ref, w_ref, t_ref, t_acc):
    step = pl.program_id(0)

    @pl.when(step == 0)
    def _():
        t_acc[...] = jnp.zeros_like(t_acc)

    w = w_ref[...].reshape(2 * BLOCK, DH)
    t_acc[:, :VOCAB] += mm(w, e_ref[...], ((0,), (1,)))
    t_acc[:, VOCAB:] += mm(w, p_ref[...], ((0,), (1,)))

    @pl.when(step == pl.num_programs(0) - 1)
    def _():
        t_ref[...] = t_acc[...].astype(BF16)


def project_tables(embed_table, position_table, w_block):
    return pl.pallas_call(
        table_kernel,
        grid=(ROWS // 2,),
        in_specs=[
            pl.BlockSpec((VOCAB, 2 * BLOCK), lambda k: (0, k)),
            pl.BlockSpec((SEQ, 2 * BLOCK), lambda k: (0, k)),
            pl.BlockSpec((2, BLOCK, DH), lambda k: (k, 0, 0)),
        ],
        out_specs=pl.BlockSpec((DH, TABLE), lambda k: (0, 0)),
        out_shape=jax.ShapeDtypeStruct((DH, TABLE), BF16),
        scratch_shapes=[pltpu.VMEM((DH, TABLE), F32)],
        compiler_params=pltpu.CompilerParams(vmem_limit_bytes=VMEM),
        name="project_tables",
    )(embed_table, position_table, w_block)


def scale_kernel(e_ref, p_ref, r_ref, g_acc, ee_acc, pp_acc):
    step = pl.program_id(0)

    @pl.when(step == 0)
    def _():
        g_acc[...] = jnp.zeros_like(g_acc)
        ee_acc[...] = jnp.zeros_like(ee_acc)
        pp_acc[...] = jnp.zeros_like(pp_acc)

    e, p = e_ref[...], p_ref[...]
    g_acc[...] += mm(e, p, ((1,), (1,)))
    pp_acc[...] += mm(p, p, ((1,), (1,)))
    wide = e.astype(F32)
    square = wide * wide
    folded = square[:, :128]
    for k in range(1, 2 * BLOCK // 128):
        folded += square[:, 128 * k : 128 * (k + 1)]
    ee_acc[...] += folded

    @pl.when(step == pl.num_programs(0) - 1)
    def _():
        ee = jnp.sum(ee_acc[...], axis=1, keepdims=True)
        diagonal = lax.broadcasted_iota(jnp.int32, (SEQ, SEQ), 0) == lax.broadcasted_iota(
            jnp.int32, (SEQ, SEQ), 1
        )
        pp = jnp.sum(jnp.where(diagonal, pp_acc[...], 0.0), axis=0, keepdims=True)
        total = jnp.maximum(ee + 2.0 * g_acc[...] + pp, 0.0)
        r_ref[...] = lax.rsqrt(total * (1.0 / D) + 1e-05)


def norm_scales(embed_table, position_table):
    return pl.pallas_call(
        scale_kernel,
        grid=(ROWS // 2,),
        in_specs=[
            pl.BlockSpec((VOCAB, 2 * BLOCK), lambda k: (0, k)),
            pl.BlockSpec((SEQ, 2 * BLOCK), lambda k: (0, k)),
        ],
        out_specs=pl.BlockSpec((VOCAB, SEQ), lambda k: (0, 0)),
        out_shape=jax.ShapeDtypeStruct((VOCAB, SEQ), F32),
        scratch_shapes=[
            pltpu.VMEM((VOCAB, SEQ), F32),
            pltpu.VMEM((VOCAB, 128), F32),
            pltpu.VMEM((SEQ, SEQ), F32),
        ],
        compiler_params=pltpu.CompilerParams(vmem_limit_bytes=VMEM),
        cost_estimate=pl.CostEstimate(flops=2 * TABLE * SEQ * D, transcendentals=VOCAB * SEQ, bytes_accessed=2 * TABLE * D),
        name="norm_scales",
    )(embed_table, position_table)


def residual_kernel(info_ref, place_ref, ids_ref, e_ref, p_ref, out_ref):
    slot = pl.program_id(0)

    @pl.when(slot < info_ref[SLOTS])
    def _():
        hit = lax.broadcasted_iota(jnp.int32, (VOCAB, SEQ), 0) == ids_ref[pl.ds(slot, 1), :]
        pick = jnp.where(hit, 1.0, 0.0).astype(BF16)
        stored = mm(pick, e_ref[...], ((0,), (0,))) + p_ref[...].astype(F32)
        out_ref[0] = stored.astype(BF16)

    @pl.when(slot >= info_ref[SLOTS])
    def _():
        out_ref[...] = jnp.zeros_like(out_ref)


def residual(info, place, ids, embed_table, position_table):
    return pl.pallas_call(
        residual_kernel,
        grid_spec=pltpu.PrefetchScalarGridSpec(
            num_scalar_prefetch=2,
            grid=(SLOTS,),
            in_specs=[
                pl.BlockSpec((SLOTS, SEQ), lambda s, *_: (0, 0)),
                pl.BlockSpec((VOCAB, FEATURES), lambda s, info, place: (0, place[1])),
                pl.BlockSpec((SEQ, FEATURES), lambda s, info, place: (0, place[1])),
            ],
            out_specs=pl.BlockSpec((1, SEQ, FEATURES), lambda s, *_: (s, 0, 0)),
        ),
        out_shape=jax.ShapeDtypeStruct((SLOTS, SEQ, FEATURES), BF16),
        compiler_params=pltpu.CompilerParams(vmem_limit_bytes=VMEM),
        cost_estimate=pl.CostEstimate(flops=2 * SLOTS * SEQ * VOCAB * FEATURES, transcendentals=0, bytes_accessed=4 * SLOTS * SEQ * FEATURES),
        name="residual",
    )(info, place, ids, embed_table, position_table)


def attend_kernel(lens_ref, info_ref, place_ref, ids_ref, r_ref, *refs):
    a_refs, b_refs = refs[:SIDE], refs[SIDE : 2 * SIDE]
    out_ref, table_ref = refs[2 * SIDE :]
    step = pl.program_id(0)
    z, x = place_ref[0] // SIDE, place_ref[0] % SIDE

    @pl.when(step == 0)
    def _():
        for dz in range(SIDE):
            for dx in range(SIDE):
                source = SIDE * ((z + SIDE - dz) % SIDE) + (x + SIDE - dx) % SIDE
                table_ref[pl.ds(source, 1), :HALF] = a_refs[dz][dx : dx + 1]
                table_ref[pl.ds(source, 1), HALF:] = b_refs[dx][dz : dz + 1]

    @pl.when(2 * step >= info_ref[SLOTS])
    def _():
        out_ref[...] = jnp.zeros_like(out_ref)

    @pl.when(2 * step < info_ref[SLOTS])
    def _():
        vocab = lax.broadcasted_iota(jnp.int32, (VOCAB, SEQ), 0)
        eye = lax.broadcasted_iota(jnp.int32, (SEQ, SEQ), 0) == lax.broadcasted_iota(
            jnp.int32, (SEQ, SEQ), 1
        )
        picks, scales = [], []
        for s in range(2):
            hit = vocab == ids_ref[pl.ds(2 * step + s, 1), :]
            scales.append(jnp.sum(jnp.where(hit, r_ref[...], 0.0), axis=0, keepdims=True))
            picks.append(
                jnp.concatenate(
                    [jnp.where(hit, 1.0, 0.0).astype(BF16), jnp.where(eye, 1.0, 0.0).astype(BF16)], 0
                )
            )
        pick = jnp.concatenate(picks, axis=1)
        scale = jnp.concatenate(scales, axis=1)
        table = table_ref[: 3 * HEADS].reshape(3 * HEADS * DH, TABLE)
        rows = (mm(table, pick, ((1,), (0,))) * scale).astype(BF16)
        key_at = lax.broadcasted_iota(jnp.int32, (SEQ, SEQ), 0)
        for s in range(2):
            valid = key_at < lens_ref[2 * step + s]
            cols = slice(SEQ * s, SEQ * (s + 1))
            for h in range(HEADS):
                q = rows[DH * h : DH * (h + 1), cols]
                k = rows[DH * (HEADS + h) : DH * (HEADS + h + 1), cols]
                v = rows[DH * (2 * HEADS + h) : DH * (2 * HEADS + h + 1), cols]
                scores = mm(k, q, ((0,), (0,))) * DH ** (-0.5)
                scores = jnp.where(valid, scores, -1e30)
                expo = jnp.exp(scores - jnp.max(scores, axis=0, keepdims=True))
                weights = (expo / jnp.sum(expo, axis=0, keepdims=True)).astype(BF16)
                mixed = mm(v, weights, ((1,), (0,)))
                out_ref[cols, DH * h : DH * (h + 1)] = mixed.T.astype(BF16)


def attend(capacity, lengths, info, place, ids, r, a_parts, b_parts):
    quarter = pl.BlockSpec((SIDE, HALF, TABLE), lambda i, *_: (0, 0, 0))
    return pl.pallas_call(
        attend_kernel,
        grid_spec=pltpu.PrefetchScalarGridSpec(
            num_scalar_prefetch=3,
            grid=(SLOTS // 2,),
            in_specs=[
                pl.BlockSpec((SLOTS, SEQ), lambda i, *_: (0, 0)),
                pl.BlockSpec((VOCAB, SEQ), lambda i, *_: (0, 0)),
                *[quarter] * (2 * SIDE),
            ],
            out_specs=pl.BlockSpec((2 * SEQ, FEATURES), lambda i, *_: (i, 0)),
            scratch_shapes=[
                pltpu.VMEM((ROWS, DH, TABLE), BF16),
            ],
        ),
        out_shape=jax.ShapeDtypeStruct((capacity, FEATURES), BF16),
        compiler_params=pltpu.CompilerParams(vmem_limit_bytes=VMEM),
        name="attend",
    )(lengths, info, place, ids, r, *a_parts, *b_parts)


def product(a_ref, other_ref, w_ref, w_other_ref):
    mine = mm(a_ref[...], w_ref[...].reshape(FEATURES, FEATURES), ((1,), (1,)))
    theirs = jnp.concatenate([w_other_ref[1], w_other_ref[0]], axis=0)
    return mine + mm(other_ref[...], theirs, ((1,), (1,)))


def pick(ahead):
    def block(place, core):
        return 2 * ((place[3] + ahead) % SIDE) + core

    shape = (2, BLOCK, FEATURES)
    return [
        pl.BlockSpec(shape, lambda i, place: (block(place, place[2]), 0, 0)),
        pl.BlockSpec(shape, lambda i, place: (block(place, 1 - place[2]), 0, 0)),
    ]


def far_kernel(place_ref, a_ref, other_ref, w_ref, w_other_ref, top_ref, bottom_ref):
    half = pl.program_id(0)
    total = product(a_ref, other_ref, w_ref, w_other_ref).astype(BF16)

    @pl.when(half == 0)
    def _():
        top_ref[...] = total

    @pl.when(half == 1)
    def _():
        bottom_ref[...] = total


def far_partials(place, mixed, other, w):
    tile = mixed.shape[0] // 2
    rows = pl.BlockSpec((tile, FEATURES), lambda i, place: (i, 0))
    whole = pl.BlockSpec((tile, FEATURES), lambda i, place: (0, 0))
    return pl.pallas_call(
        far_kernel,
        grid_spec=pltpu.PrefetchScalarGridSpec(
            num_scalar_prefetch=1,
            grid=(2,),
            in_specs=[rows, rows, *pick(2)],
            out_specs=[whole, whole],
        ),
        out_shape=[jax.ShapeDtypeStruct((tile, FEATURES), BF16)] * 2,
        compiler_params=pltpu.CompilerParams(vmem_limit_bytes=VMEM),
        name="far_partials",
    )(place, mixed, other, w, w)


def free_kernel(place_ref, a0, o0, a1, o1, w0, w1, w2, w3, up_ref, down_ref):
    up_ref[...] = product(a1, o1, w0, w1).astype(BF16)
    down_ref[...] = product(a0, o0, w2, w3).astype(BF16)


def free_partials(place, mixed, other, w):
    tile = mixed.shape[0] // 2
    first = pl.BlockSpec((tile, FEATURES), lambda i, place: (0, 0))
    second = pl.BlockSpec((tile, FEATURES), lambda i, place: (1, 0))
    return pl.pallas_call(
        free_kernel,
        grid_spec=pltpu.PrefetchScalarGridSpec(
            num_scalar_prefetch=1,
            grid=(1,),
            in_specs=[first, first, second, second, *pick(1), *pick(3)],
            out_specs=[first, first],
        ),
        out_shape=[jax.ShapeDtypeStruct((tile, FEATURES), BF16)] * 2,
        compiler_params=pltpu.CompilerParams(vmem_limit_bytes=VMEM),
        name="free_partials",
    )(place, mixed, other, mixed, other, w, w, w, w)


def relay_kernel(place_ref, a0, o0, a1, o1, w0, w1, w2, w3, from_below, from_above, up_ref, down_ref):
    up_ref[...] = (product(a0, o0, w0, w1) + from_below[...].astype(F32)).astype(BF16)
    down_ref[...] = (product(a1, o1, w2, w3) + from_above[...].astype(F32)).astype(BF16)


def relay_partials(place, mixed, other, w, from_below, from_above):
    tile = mixed.shape[0] // 2
    first = pl.BlockSpec((tile, FEATURES), lambda i, place: (0, 0))
    second = pl.BlockSpec((tile, FEATURES), lambda i, place: (1, 0))
    return pl.pallas_call(
        relay_kernel,
        grid_spec=pltpu.PrefetchScalarGridSpec(
            num_scalar_prefetch=1,
            grid=(1,),
            in_specs=[first, first, second, second, *pick(1), *pick(3), first, first],
            out_specs=[first, first],
        ),
        out_shape=[jax.ShapeDtypeStruct((tile, FEATURES), BF16)] * 2,
        compiler_params=pltpu.CompilerParams(vmem_limit_bytes=VMEM),
        name="relay_partials",
    )(place, mixed, other, mixed, other, w, w, w, w, from_below, from_above)


def base_kernel(place_ref, a_ref, other_ref, w_ref, w_other_ref, out_ref):
    out_ref[...] = product(a_ref, other_ref, w_ref, w_other_ref)


def base_partial(place, mixed, other, w):
    tokens = mixed.shape[0]
    rows = pl.BlockSpec((tokens // 2, FEATURES), lambda i, place: (i, 0))
    return pl.pallas_call(
        base_kernel,
        grid_spec=pltpu.PrefetchScalarGridSpec(
            num_scalar_prefetch=1,
            grid=(2,),
            in_specs=[rows, rows, *pick(0)],
            out_specs=rows,
        ),
        out_shape=jax.ShapeDtypeStruct((tokens, FEATURES), F32),
        compiler_params=pltpu.CompilerParams(vmem_limit_bytes=VMEM),
        name="base_partial",
    )(place, mixed, other, w, w)


def finish_kernel(lens_ref, info_ref, stored_ref, base_ref, *refs):
    below, above, out_ref = refs[:2], refs[2:4], refs[4]
    slot = pl.program_id(0)
    live = slot < info_ref[SLOTS]
    for half in range(2):
        here = (slot >= SLOTS // 2) if half else (slot < SLOTS // 2)

        @pl.when(live & here)
        def _(half=half):
            total = base_ref[...] + below[half][...].astype(F32) + above[half][...].astype(F32)
            valid = lax.broadcasted_iota(jnp.int32, (SEQ, FEATURES), 0) < lens_ref[slot]
            result = stored_ref[0].astype(F32) + total
            out_ref[0] = jnp.where(valid, result, 0.0).astype(BF16)

    @pl.when(jnp.logical_not(live))
    def _():
        out_ref[...] = jnp.zeros_like(out_ref)


def finish(lengths, info, stored, base, below, above):
    high = pl.BlockSpec((SEQ, FEATURES), lambda s, *_: (jnp.minimum(s, SLOTS // 2 - 1), 0))
    low = pl.BlockSpec((SEQ, FEATURES), lambda s, *_: (jnp.maximum(s - SLOTS // 2, 0), 0))
    one = pl.BlockSpec((1, SEQ, FEATURES), lambda s, *_: (s, 0, 0))
    return pl.pallas_call(
        finish_kernel,
        grid_spec=pltpu.PrefetchScalarGridSpec(
            num_scalar_prefetch=2,
            grid=(SLOTS,),
            in_specs=[one, pl.BlockSpec((SEQ, FEATURES), lambda s, *_: (s, 0)), high, low, high, low],
            out_specs=one,
        ),
        out_shape=jax.ShapeDtypeStruct((SLOTS, SEQ, FEATURES), BF16),
        compiler_params=pltpu.CompilerParams(vmem_limit_bytes=VMEM),
        name="finish",
    )(lengths, info, stored, base, *below, *above)


def on_device(
    token_ids,
    set_lengths,
    live_counts,
    embed_table,
    position_table,
    norm_gain,
    w_query,
    w_key,
    w_value,
    w_out,
):
    row = lax.axis_index("row")
    part = lax.axis_index("mp")
    y, core = part // 2, part % 2
    place = jnp.stack([row, part, core, y])

    def shifted(o, along_x):
        pairs = []
        for z in range(SIDE):
            for x in range(SIDE):
                to = SIDE * z + (x + o) % SIDE if along_x else SIDE * ((z + o) % SIDE) + x
                pairs.append((SIDE * z + x, to))
        return pairs

    def spread(value, along_x):
        near = {o: lax.ppermute(value, "row", shifted(o, along_x)) for o in (1, 3, 2)}
        return [value, near[1], near[2], near[3]]

    packed, info = pack(
        place, set_lengths, live_counts, norm_gain.reshape(8, 2 * BLOCK), w_query, w_key, w_value
    )
    packed, w_out, embed_late = lax.optimization_barrier((packed, w_out, embed_table))
    turned = w_out.T
    cross = []
    for z in range(SIDE):
        for x in range(SIDE):
            for line in range(SIDE):
                c = 1 - x // 2
                source = (SIDE * z + x) * 8 + 2 * line + c
                cross.append((source, (SIDE * z + 3 - x) * 8 + 2 * line + 1 - c))
    crossed = lax.ppermute(turned, ("row", "mp"), cross)
    tiles = jnp.where((row % SIDE) // 2 == core, turned, crossed)
    r = norm_scales(embed_late, position_table)
    w_block = lax.all_to_all(packed, "row", 0, 0)
    w_block, tiles, r = lax.optimization_barrier((w_block, tiles, r))
    w_all = lax.all_gather(tiles, "row", axis=0)
    mine = project_tables(embed_table, position_table, w_block)

    a_line = jnp.stack(spread(mine[:HALF], True))
    b_line = jnp.stack(spread(mine[HALF:], False))
    a_line, b_line = lax.optimization_barrier((a_line, b_line))
    a_parts, b_parts = spread(a_line, False), spread(b_line, True)
    ids_late, a_parts[1] = lax.optimization_barrier((token_ids, a_parts[1]))
    stored = residual(info, place, ids_late, embed_table, position_table)
    swap = [(2 * i + c, 2 * i + 1 - c) for i in range(SIDE) for c in range(2)]

    def along(o):
        return [(2 * i + c, 2 * ((i + o) % SIDE) + c) for i in range(SIDE) for c in range(2)]

    def rest(capacity, a_parts, b_parts, w, r):
        mixed = attend(capacity, set_lengths, info, place, token_ids, r, a_parts, b_parts)
        other = lax.ppermute(mixed, "mp", swap)
        top, bottom = far_partials(place, mixed, other, w)
        from_below = lax.ppermute(top, "mp", along(1))
        from_above = lax.ppermute(bottom, "mp", along(3))
        free_up, free_down = free_partials(place, mixed, other, w)
        below_low = lax.ppermute(free_up, "mp", along(1))
        above_high = lax.ppermute(free_down, "mp", along(3))
        up, down = relay_partials(place, mixed, other, w, from_below, from_above)
        below_high = lax.ppermute(up, "mp", along(1))
        above_low = lax.ppermute(down, "mp", along(3))
        base = base_partial(place, mixed, other, w)
        return finish(
            set_lengths, info, stored, base, (below_high, below_low), (above_high, above_low)
        )

    return rest(SLOTS * SEQ, a_parts, b_parts, w_all, r)


def solution(mesh):
    in_specs = (
        P("row", None),
        P("row"),
        P(),
        P(),
        P(),
        P(),
        P("row", "mp"),
        P("row", "mp"),
        P("row", "mp"),
        P("mp", "row"),
    )
    out_specs = P("row", None, "mp")
    return jax.shard_map(
        on_device, mesh=mesh, in_specs=in_specs, out_specs=out_specs, check_vma=False
    )
```

```python
import jax
import jax.numpy as jnp
from jax import lax
from jax.experimental import pallas as pl
from jax.experimental.pallas import tpu as pltpu
from jax.sharding import PartitionSpec as P

D = 5120
DH = 128
HEADS = 5
ROWS = 16
VOCAB = 512
SEQ = 128
SLOTS = 8
TABLE = VOCAB + SEQ
BLOCK = D // ROWS
FEATURES = 640
HALF = DH // 2
SIDE = 4
F32 = jnp.float32
BF16 = jnp.bfloat16
VMEM = 16 << 20
MOST = 57 << 20
GROUP = 16


def mm(a, b, dims):
    return lax.dot_general(a, b, (dims, ((), ())), preferred_element_type=F32)


def pack_kernel(place_ref, lens_ref, counts_ref, gain_ref, q_hbm, k_hbm, v_hbm, out_ref, info_ref, w_ref, turned_ref, sems):
    row = place_ref[0]
    copies = [
        pltpu.make_async_copy(source, w_ref.at[j], sems.at[j])
        for j, source in enumerate((q_hbm, k_hbm, v_hbm))
    ]
    for copy in copies:
        copy.start()
    live = counts_ref[row]
    total = jnp.int32(0)
    for s in range(SLOTS):
        info_ref[s] = GROUP * total
        groups = (lens_ref[s] + GROUP - 1) // GROUP
        total = total + jnp.where(s < live, groups, 0)
    info_ref[SLOTS] = live
    begin = pl.multiple_of((row // 2) * 2 * BLOCK, 2 * BLOCK)
    line = jnp.broadcast_to(gain_ref[:, pl.ds(begin, 2 * BLOCK)], (8, 2 * BLOCK))
    turned_ref[...] = line.T
    start = pl.multiple_of((row % 2) * BLOCK, 8)
    gain = turned_ref[pl.ds(start, BLOCK), :][:, :1]
    out_ref[ROWS - 1] = jnp.zeros((BLOCK, DH), BF16)
    for j, copy in enumerate(copies):
        copy.wait()
        for h in range(HEADS):
            block = gain * w_ref[j, :, DH * h : DH * (h + 1)].astype(F32)
            out_ref[HEADS * j + h] = block.astype(BF16)


def pack(place, lengths, counts, gain, w_query, w_key, w_value):
    stay = pl.BlockSpec(memory_space=pltpu.HBM)
    return pl.pallas_call(
        pack_kernel,
        grid_spec=pltpu.PrefetchScalarGridSpec(
            num_scalar_prefetch=3,
            grid=(1,),
            in_specs=[pl.BlockSpec((1, D), lambda i, *_: (0, 0)), stay, stay, stay],
            out_specs=[
                pl.BlockSpec((ROWS, BLOCK, DH), lambda i, *_: (0, 0, 0)),
                pl.BlockSpec(memory_space=pltpu.SMEM),
            ],
            scratch_shapes=[
                pltpu.VMEM((3, BLOCK, FEATURES), BF16),
                pltpu.VMEM((2 * BLOCK, 8), F32),
                pltpu.SemaphoreType.DMA((3,)),
            ],
        ),
        out_shape=[
            jax.ShapeDtypeStruct((ROWS, BLOCK, DH), BF16),
            jax.ShapeDtypeStruct((2 * SLOTS,), jnp.int32),
        ],
        compiler_params=pltpu.CompilerParams(vmem_limit_bytes=MOST),
        name="pack",
    )(place, lengths, counts, gain, w_query, w_key, w_value)


def table_kernel(e_ref, p_ref, w_ref, t_ref, t_acc):
    step = pl.program_id(0)

    @pl.when(step == 0)
    def _():
        t_acc[...] = jnp.zeros_like(t_acc)

    w = w_ref[...].reshape(2 * BLOCK, DH)
    t_acc[:, :VOCAB] += mm(w, e_ref[...], ((0,), (1,)))
    t_acc[:, VOCAB:] += mm(w, p_ref[...], ((0,), (1,)))

    @pl.when(step == pl.num_programs(0) - 1)
    def _():
        t_ref[...] = t_acc[...].astype(BF16)


def project_tables(embed_table, position_table, w_block):
    return pl.pallas_call(
        table_kernel,
        grid=(ROWS // 2,),
        in_specs=[
            pl.BlockSpec((VOCAB, 2 * BLOCK), lambda k: (0, k)),
            pl.BlockSpec((SEQ, 2 * BLOCK), lambda k: (0, k)),
            pl.BlockSpec((2, BLOCK, DH), lambda k: (k, 0, 0)),
        ],
        out_specs=pl.BlockSpec((DH, TABLE), lambda k: (0, 0)),
        out_shape=jax.ShapeDtypeStruct((DH, TABLE), BF16),
        scratch_shapes=[pltpu.VMEM((DH, TABLE), F32)],
        compiler_params=pltpu.CompilerParams(vmem_limit_bytes=VMEM),
        name="project_tables",
    )(embed_table, position_table, w_block)


def scale_kernel(e_ref, p_ref, r_ref, g_acc, ee_acc, pp_acc):
    step = pl.program_id(0)

    @pl.when(step == 0)
    def _():
        g_acc[...] = jnp.zeros_like(g_acc)
        ee_acc[...] = jnp.zeros_like(ee_acc)
        pp_acc[...] = jnp.zeros_like(pp_acc)

    e, p = e_ref[...], p_ref[...]
    g_acc[...] += mm(e, p, ((1,), (1,)))
    pp_acc[...] += mm(p, p, ((1,), (1,)))
    wide = e.astype(F32)
    square = wide * wide
    folded = square[:, :128]
    for k in range(1, 2 * BLOCK // 128):
        folded += square[:, 128 * k : 128 * (k + 1)]
    ee_acc[...] += folded

    @pl.when(step == pl.num_programs(0) - 1)
    def _():
        ee = jnp.sum(ee_acc[...], axis=1, keepdims=True)
        diagonal = lax.broadcasted_iota(jnp.int32, (SEQ, SEQ), 0) == lax.broadcasted_iota(
            jnp.int32, (SEQ, SEQ), 1
        )
        pp = jnp.sum(jnp.where(diagonal, pp_acc[...], 0.0), axis=0, keepdims=True)
        total = jnp.maximum(ee + 2.0 * g_acc[...] + pp, 0.0)
        r_ref[...] = lax.rsqrt(total * (1.0 / D) + 1e-05)


def norm_scales(embed_table, position_table):
    return pl.pallas_call(
        scale_kernel,
        grid=(ROWS // 2,),
        in_specs=[
            pl.BlockSpec((VOCAB, 2 * BLOCK), lambda k: (0, k)),
            pl.BlockSpec((SEQ, 2 * BLOCK), lambda k: (0, k)),
        ],
        out_specs=pl.BlockSpec((VOCAB, SEQ), lambda k: (0, 0)),
        out_shape=jax.ShapeDtypeStruct((VOCAB, SEQ), F32),
        scratch_shapes=[
            pltpu.VMEM((VOCAB, SEQ), F32),
            pltpu.VMEM((VOCAB, 128), F32),
            pltpu.VMEM((SEQ, SEQ), F32),
        ],
        compiler_params=pltpu.CompilerParams(vmem_limit_bytes=VMEM),
        cost_estimate=pl.CostEstimate(flops=2 * TABLE * SEQ * D, transcendentals=VOCAB * SEQ, bytes_accessed=2 * TABLE * D),
        name="norm_scales",
    )(embed_table, position_table)


def residual_kernel(info_ref, place_ref, ids_ref, e_ref, p_ref, out_ref):
    slot = pl.program_id(0)

    @pl.when(slot < info_ref[SLOTS])
    def _():
        hit = lax.broadcasted_iota(jnp.int32, (VOCAB, SEQ), 0) == ids_ref[pl.ds(slot, 1), :]
        pick = jnp.where(hit, 1.0, 0.0).astype(BF16)
        stored = mm(pick, e_ref[...], ((0,), (0,))) + p_ref[...].astype(F32)
        out_ref[0] = stored.astype(BF16)

    @pl.when(slot >= info_ref[SLOTS])
    def _():
        out_ref[...] = jnp.zeros_like(out_ref)


def residual(info, place, ids, embed_table, position_table):
    return pl.pallas_call(
        residual_kernel,
        grid_spec=pltpu.PrefetchScalarGridSpec(
            num_scalar_prefetch=2,
            grid=(SLOTS,),
            in_specs=[
                pl.BlockSpec((SLOTS, SEQ), lambda s, *_: (0, 0)),
                pl.BlockSpec((VOCAB, FEATURES), lambda s, info, place: (0, place[1])),
                pl.BlockSpec((SEQ, FEATURES), lambda s, info, place: (0, place[1])),
            ],
            out_specs=pl.BlockSpec((1, SEQ, FEATURES), lambda s, *_: (s, 0, 0)),
        ),
        out_shape=jax.ShapeDtypeStruct((SLOTS, SEQ, FEATURES), BF16),
        compiler_params=pltpu.CompilerParams(vmem_limit_bytes=VMEM),
        cost_estimate=pl.CostEstimate(flops=2 * SLOTS * SEQ * VOCAB * FEATURES, transcendentals=0, bytes_accessed=4 * SLOTS * SEQ * FEATURES),
        name="residual",
    )(info, place, ids, embed_table, position_table)


def attend_kernel(lens_ref, info_ref, place_ref, ids_ref, r_ref, *refs):
    a_refs, b_refs = refs[:SIDE], refs[SIDE : 2 * SIDE]
    out_ref, table_ref = refs[2 * SIDE :]
    step = pl.program_id(0)
    z, x = place_ref[0] // SIDE, place_ref[0] % SIDE

    @pl.when(step == 0)
    def _():
        for dz in range(SIDE):
            for dx in range(SIDE):
                source = SIDE * ((z + SIDE - dz) % SIDE) + (x + SIDE - dx) % SIDE
                table_ref[pl.ds(source, 1), :HALF] = a_refs[dz][dx : dx + 1]
                table_ref[pl.ds(source, 1), HALF:] = b_refs[dx][dz : dz + 1]

    @pl.when(2 * step >= info_ref[SLOTS])
    def _():
        out_ref[...] = jnp.zeros_like(out_ref)

    @pl.when(2 * step < info_ref[SLOTS])
    def _():
        vocab = lax.broadcasted_iota(jnp.int32, (VOCAB, SEQ), 0)
        eye = lax.broadcasted_iota(jnp.int32, (SEQ, SEQ), 0) == lax.broadcasted_iota(
            jnp.int32, (SEQ, SEQ), 1
        )
        picks, scales = [], []
        for s in range(2):
            hit = vocab == ids_ref[pl.ds(2 * step + s, 1), :]
            scales.append(jnp.sum(jnp.where(hit, r_ref[...], 0.0), axis=0, keepdims=True))
            picks.append(
                jnp.concatenate(
                    [jnp.where(hit, 1.0, 0.0).astype(BF16), jnp.where(eye, 1.0, 0.0).astype(BF16)], 0
                )
            )
        pick = jnp.concatenate(picks, axis=1)
        scale = jnp.concatenate(scales, axis=1)
        table = table_ref[: 3 * HEADS].reshape(3 * HEADS * DH, TABLE)
        rows = (mm(table, pick, ((1,), (0,))) * scale).astype(BF16)
        key_at = lax.broadcasted_iota(jnp.int32, (SEQ, SEQ), 0)
        for s in range(2):
            valid = key_at < lens_ref[2 * step + s]
            cols = slice(SEQ * s, SEQ * (s + 1))
            for h in range(HEADS):
                q = rows[DH * h : DH * (h + 1), cols]
                k = rows[DH * (HEADS + h) : DH * (HEADS + h + 1), cols]
                v = rows[DH * (2 * HEADS + h) : DH * (2 * HEADS + h + 1), cols]
                scores = mm(k, q, ((0,), (0,))) * DH ** (-0.5)
                scores = jnp.where(valid, scores, -1e30)
                expo = jnp.exp(scores - jnp.max(scores, axis=0, keepdims=True))
                weights = (expo / jnp.sum(expo, axis=0, keepdims=True)).astype(BF16)
                mixed = mm(v, weights, ((1,), (0,)))
                out_ref[cols, DH * h : DH * (h + 1)] = mixed.T.astype(BF16)


def attend(capacity, lengths, info, place, ids, r, a_parts, b_parts):
    quarter = pl.BlockSpec((SIDE, HALF, TABLE), lambda i, *_: (0, 0, 0))
    return pl.pallas_call(
        attend_kernel,
        grid_spec=pltpu.PrefetchScalarGridSpec(
            num_scalar_prefetch=3,
            grid=(SLOTS // 2,),
            in_specs=[
                pl.BlockSpec((SLOTS, SEQ), lambda i, *_: (0, 0)),
                pl.BlockSpec((VOCAB, SEQ), lambda i, *_: (0, 0)),
                *[quarter] * (2 * SIDE),
            ],
            out_specs=pl.BlockSpec((2 * SEQ, FEATURES), lambda i, *_: (i, 0)),
            scratch_shapes=[
                pltpu.VMEM((ROWS, DH, TABLE), BF16),
            ],
        ),
        out_shape=jax.ShapeDtypeStruct((capacity, FEATURES), BF16),
        compiler_params=pltpu.CompilerParams(vmem_limit_bytes=VMEM),
        name="attend",
    )(lengths, info, place, ids, r, *a_parts, *b_parts)


def product(a_ref, other_ref, w_ref, w_other_ref):
    mine = mm(a_ref[...], w_ref[...].reshape(FEATURES, FEATURES), ((1,), (1,)))
    theirs = jnp.concatenate([w_other_ref[1], w_other_ref[0]], axis=0)
    return mine + mm(other_ref[...], theirs, ((1,), (1,)))


def pick(ahead):
    def block(place, core):
        return 2 * ((place[3] + ahead) % SIDE) + core

    shape = (2, BLOCK, FEATURES)
    return [
        pl.BlockSpec(shape, lambda i, place: (block(place, place[2]), 0, 0)),
        pl.BlockSpec(shape, lambda i, place: (block(place, 1 - place[2]), 0, 0)),
    ]


def far_kernel(place_ref, a_ref, other_ref, w_ref, w_other_ref, top_ref, bottom_ref):
    half = pl.program_id(0)
    total = product(a_ref, other_ref, w_ref, w_other_ref).astype(BF16)

    @pl.when(half == 0)
    def _():
        top_ref[...] = total

    @pl.when(half == 1)
    def _():
        bottom_ref[...] = total


def far_partials(place, mixed, other, w):
    tile = mixed.shape[0] // 2
    rows = pl.BlockSpec((tile, FEATURES), lambda i, place: (i, 0))
    whole = pl.BlockSpec((tile, FEATURES), lambda i, place: (0, 0))
    return pl.pallas_call(
        far_kernel,
        grid_spec=pltpu.PrefetchScalarGridSpec(
            num_scalar_prefetch=1,
            grid=(2,),
            in_specs=[rows, rows, *pick(2)],
            out_specs=[whole, whole],
        ),
        out_shape=[jax.ShapeDtypeStruct((tile, FEATURES), BF16)] * 2,
        compiler_params=pltpu.CompilerParams(vmem_limit_bytes=VMEM),
        name="far_partials",
    )(place, mixed, other, w, w)


def free_kernel(place_ref, a0, o0, a1, o1, w0, w1, w2, w3, up_ref, down_ref):
    up_ref[...] = product(a1, o1, w0, w1).astype(BF16)
    down_ref[...] = product(a0, o0, w2, w3).astype(BF16)


def free_partials(place, mixed, other, w):
    tile = mixed.shape[0] // 2
    first = pl.BlockSpec((tile, FEATURES), lambda i, place: (0, 0))
    second = pl.BlockSpec((tile, FEATURES), lambda i, place: (1, 0))
    return pl.pallas_call(
        free_kernel,
        grid_spec=pltpu.PrefetchScalarGridSpec(
            num_scalar_prefetch=1,
            grid=(1,),
            in_specs=[first, first, second, second, *pick(1), *pick(3)],
            out_specs=[first, first],
        ),
        out_shape=[jax.ShapeDtypeStruct((tile, FEATURES), BF16)] * 2,
        compiler_params=pltpu.CompilerParams(vmem_limit_bytes=VMEM),
        name="free_partials",
    )(place, mixed, other, mixed, other, w, w, w, w)


def relay_kernel(place_ref, a0, o0, a1, o1, w0, w1, w2, w3, from_below, from_above, up_ref, down_ref):
    up_ref[...] = (product(a0, o0, w0, w1) + from_below[...].astype(F32)).astype(BF16)
    down_ref[...] = (product(a1, o1, w2, w3) + from_above[...].astype(F32)).astype(BF16)


def relay_partials(place, mixed, other, w, from_below, from_above):
    tile = mixed.shape[0] // 2
    first = pl.BlockSpec((tile, FEATURES), lambda i, place: (0, 0))
    second = pl.BlockSpec((tile, FEATURES), lambda i, place: (1, 0))
    return pl.pallas_call(
        relay_kernel,
        grid_spec=pltpu.PrefetchScalarGridSpec(
            num_scalar_prefetch=1,
            grid=(1,),
            in_specs=[first, first, second, second, *pick(1), *pick(3), first, first],
            out_specs=[first, first],
        ),
        out_shape=[jax.ShapeDtypeStruct((tile, FEATURES), BF16)] * 2,
        compiler_params=pltpu.CompilerParams(vmem_limit_bytes=VMEM),
        name="relay_partials",
    )(place, mixed, other, mixed, other, w, w, w, w, from_below, from_above)


def base_kernel(place_ref, a_ref, other_ref, w_ref, w_other_ref, out_ref):
    out_ref[...] = product(a_ref, other_ref, w_ref, w_other_ref)


def base_partial(place, mixed, other, w):
    tokens = mixed.shape[0]
    rows = pl.BlockSpec((tokens // 2, FEATURES), lambda i, place: (i, 0))
    return pl.pallas_call(
        base_kernel,
        grid_spec=pltpu.PrefetchScalarGridSpec(
            num_scalar_prefetch=1,
            grid=(2,),
            in_specs=[rows, rows, *pick(0)],
            out_specs=rows,
        ),
        out_shape=jax.ShapeDtypeStruct((tokens, FEATURES), F32),
        compiler_params=pltpu.CompilerParams(vmem_limit_bytes=VMEM),
        name="base_partial",
    )(place, mixed, other, w, w)


def finish_kernel(lens_ref, info_ref, stored_ref, base_ref, *refs):
    below, above, out_ref = refs[:2], refs[2:4], refs[4]
    slot = pl.program_id(0)
    live = slot < info_ref[SLOTS]
    for half in range(2):
        here = (slot >= SLOTS // 2) if half else (slot < SLOTS // 2)

        @pl.when(live & here)
        def _(half=half):
            total = base_ref[...] + below[half][...].astype(F32) + above[half][...].astype(F32)
            valid = lax.broadcasted_iota(jnp.int32, (SEQ, FEATURES), 0) < lens_ref[slot]
            result = stored_ref[0].astype(F32) + total
            out_ref[0] = jnp.where(valid, result, 0.0).astype(BF16)

    @pl.when(jnp.logical_not(live))
    def _():
        out_ref[...] = jnp.zeros_like(out_ref)


def finish(lengths, info, stored, base, below, above):
    high = pl.BlockSpec((SEQ, FEATURES), lambda s, *_: (jnp.minimum(s, SLOTS // 2 - 1), 0))
    low = pl.BlockSpec((SEQ, FEATURES), lambda s, *_: (jnp.maximum(s - SLOTS // 2, 0), 0))
    one = pl.BlockSpec((1, SEQ, FEATURES), lambda s, *_: (s, 0, 0))
    return pl.pallas_call(
        finish_kernel,
        grid_spec=pltpu.PrefetchScalarGridSpec(
            num_scalar_prefetch=2,
            grid=(SLOTS,),
            in_specs=[one, pl.BlockSpec((SEQ, FEATURES), lambda s, *_: (s, 0)), high, low, high, low],
            out_specs=one,
        ),
        out_shape=jax.ShapeDtypeStruct((SLOTS, SEQ, FEATURES), BF16),
        compiler_params=pltpu.CompilerParams(vmem_limit_bytes=VMEM),
        name="finish",
    )(lengths, info, stored, base, *below, *above)


def on_device(
    token_ids,
    set_lengths,
    live_counts,
    embed_table,
    position_table,
    norm_gain,
    w_query,
    w_key,
    w_value,
    w_out,
):
    row = lax.axis_index("row")
    part = lax.axis_index("mp")
    y, core = part // 2, part % 2
    place = jnp.stack([row, part, core, y])

    def shifted(o, along_x):
        pairs = []
        for z in range(SIDE):
            for x in range(SIDE):
                to = SIDE * z + (x + o) % SIDE if along_x else SIDE * ((z + o) % SIDE) + x
                pairs.append((SIDE * z + x, to))
        return pairs

    def spread(value, along_x):
        near = {o: lax.ppermute(value, "row", shifted(o, along_x)) for o in (1, 3, 2)}
        return [value, near[1], near[2], near[3]]

    packed, info = pack(
        place, set_lengths, live_counts, norm_gain.reshape(1, D), w_query, w_key, w_value
    )
    packed, w_out, embed_late = lax.optimization_barrier((packed, w_out, embed_table))
    turned = w_out.T
    cross = []
    for z in range(SIDE):
        for x in range(SIDE):
            for line in range(SIDE):
                c = 1 - x // 2
                source = (SIDE * z + x) * 8 + 2 * line + c
                cross.append((source, (SIDE * z + 3 - x) * 8 + 2 * line + 1 - c))
    crossed = lax.ppermute(turned, ("row", "mp"), cross)
    tiles = jnp.where((row % SIDE) // 2 == core, turned, crossed)
    r = norm_scales(embed_late, position_table)
    w_block = lax.all_to_all(packed, "row", 0, 0)
    w_block, tiles, r = lax.optimization_barrier((w_block, tiles, r))
    w_all = lax.all_gather(tiles, "row", axis=0)
    mine = project_tables(embed_table, position_table, w_block)

    a_line = jnp.stack(spread(mine[:HALF], True))
    b_line = jnp.stack(spread(mine[HALF:], False))
    a_line, b_line = lax.optimization_barrier((a_line, b_line))
    a_parts, b_parts = spread(a_line, False), spread(b_line, True)
    ids_late, a_parts[1] = lax.optimization_barrier((token_ids, a_parts[1]))
    stored = residual(info, place, ids_late, embed_table, position_table)
    swap = [(2 * i + c, 2 * i + 1 - c) for i in range(SIDE) for c in range(2)]

    def along(o):
        return [(2 * i + c, 2 * ((i + o) % SIDE) + c) for i in range(SIDE) for c in range(2)]

    def rest(capacity, a_parts, b_parts, w, r):
        mixed = attend(capacity, set_lengths, info, place, token_ids, r, a_parts, b_parts)
        other = lax.ppermute(mixed, "mp", swap)
        top, bottom = far_partials(place, mixed, other, w)
        from_below = lax.ppermute(top, "mp", along(1))
        from_above = lax.ppermute(bottom, "mp", along(3))
        free_up, free_down = free_partials(place, mixed, other, w)
        below_low = lax.ppermute(free_up, "mp", along(1))
        above_high = lax.ppermute(free_down, "mp", along(3))
        up, down = relay_partials(place, mixed, other, w, from_below, from_above)
        below_high = lax.ppermute(up, "mp", along(1))
        above_low = lax.ppermute(down, "mp", along(3))
        base = base_partial(place, mixed, other, w)
        return finish(
            set_lengths, info, stored, base, (below_high, below_low), (above_high, above_low)
        )

    return rest(SLOTS * SEQ, a_parts, b_parts, w_all, r)


def solution(mesh):
    in_specs = (
        P("row", None),
        P("row"),
        P(),
        P(),
        P(),
        P(),
        P("row", "mp"),
        P("row", "mp"),
        P("row", "mp"),
        P("mp", "row"),
    )
    out_specs = P("row", None, "mp")
    return jax.shard_map(
        on_device, mesh=mesh, in_specs=in_specs, out_specs=out_specs, check_vma=False
    )
```
